128 devices in a mesh: cells: 128 (over x, z, y, core).
Axes of the slice: x: 4, y: 4, z: 4, core: 2. Of those that a mesh axis runs over, the one named last changes fastest.
Arguments:
- src_feat: bfloat16 [2048, 32, 256], P('cells'), may hold values from -16 to 16
- tgt_feat: bfloat16 [2048, 32, 256], P('cells'), may hold values from -16 to 16
- src_len: int32 [2048], P('cells'), may hold values from 64 to 256, as said below
- tgt_len: int32 [2048], P('cells'), may hold values from 64 to 256, as said below
- neighbours: int32 [2048, 5], P('cells'), may hold values from 0 to 2047, as said below
Outputs:
- source_pot: float32 [2048, 256], P('cells')
- target_pot: float32 [2048, 256], P('cells')
The draws below stay inside these ranges and needn't reach their ends.
Inputs may be any that keep to these rules, and one draw needn't show every extreme that they name: `src_len`: some cell holds 256 live points. `tgt_len`: some cell holds 256 live points. `neighbours`: cell c lies on device c // 16. The five cells of a row lie on five different devices, none of them the row's own. Of all entries in the rows of one device, at most 1 name cells of any one device, and in every draw some device has 1 entries naming one device.
All inputs are finite; a program needn't handle non-finite values.
Results may differ from the reference program's by a relative error of at most 0.0005.
Values may be sent and summed in bfloat16 or wider, within the bound.
A program may use at most 64 MiB of HBM per device.

```python
import jax
import jax.numpy as jnp
from jax import lax

FEAT = 32
PTS = 256
CELLS_DEV = 16
ITERS = 2
CELLS = 2048


def feature_cloud(key, which):
    noise = jax.random.normal(jax.random.fold_in(key, which), (CELLS, FEAT, PTS), jnp.float32)
    values = 0.3 * noise
    return jnp.clip(values, -16.0, 16.0)


def draw_src_feat(key, part):
    return feature_cloud(key, 1).astype(jnp.bfloat16)


def draw_tgt_feat(key, part):
    return feature_cloud(key, 2).astype(jnp.bfloat16)


def cell_lengths(key):
    counts = jax.random.randint(key, (CELLS,), PTS // 4, PTS + 1, jnp.int32)
    full_cell = jax.random.randint(jax.random.fold_in(key, 1), (), 0, CELLS, jnp.int32)
    return jnp.where(jnp.arange(CELLS, dtype=jnp.int32) == full_cell, PTS, counts).astype(jnp.int32)


def draw_src_len(key, part):
    return cell_lengths(jax.random.fold_in(key, 21))


def draw_tgt_len(key, part):
    return cell_lengths(jax.random.fold_in(key, 22))


def draw_neighbours(key, part):
    devices = CELLS // CELLS_DEV
    entries = 5 * CELLS_DEV
    device_keys = jax.random.split(jax.random.fold_in(key, 31), devices)
    orders = jax.vmap(lambda device_key: jax.random.permutation(device_key, devices - 1))(device_keys)
    column = jnp.arange(entries, dtype=jnp.int32) % (devices - 1)
    owners = (jnp.arange(devices, dtype=jnp.int32)[:, None] + 1 + orders[:, column]) % devices
    spot = jax.random.randint(jax.random.fold_in(key, 32), (devices, entries), 0, CELLS_DEV, jnp.int32)
    return (owners * CELLS_DEV + spot).reshape(CELLS, 5).astype(jnp.int32)


def setup_inputs(seed: int = 0) -> dict:
    keys = jax.random.split(jax.random.key(seed), 6)
    src_feat = draw_src_feat(jax.random.fold_in(keys[5], 71), 0)
    tgt_feat = draw_tgt_feat(jax.random.fold_in(keys[5], 71), 0)
    src_len = draw_src_len(jax.random.fold_in(keys[5], 71), 0)
    tgt_len = draw_tgt_len(jax.random.fold_in(keys[5], 71), 0)
    neighbours = draw_neighbours(jax.random.fold_in(keys[5], 71), 0)
    return {"src_feat": src_feat, "tgt_feat": tgt_feat, "src_len": src_len, "tgt_len": tgt_len, "neighbours": neighbours}


entropy_scale = 0.5
marginal_weight = 1.0
damping = marginal_weight / (marginal_weight + entropy_scale)
masked_score = -1.0e30


def live_points(lengths):
    return lax.broadcasted_iota(jnp.int32, (lengths.shape[0], PTS), 1) < lengths[:, None]


def pair_costs(source_block, target_block):
    cross = lax.dot_general(source_block, target_block, (((0,), (0,)), ((), ())), preferred_element_type=jnp.float32)
    source_wide = source_block.astype(jnp.float32)
    target_wide = target_block.astype(jnp.float32)
    return (0.5 * jnp.sum(source_wide * source_wide, axis=0)[:, None] + 0.5 * jnp.sum(target_wide * target_wide, axis=0)[None, :]) - cross


def gathered_targets(tgt_feat, row_cells):
    return jnp.transpose(tgt_feat[row_cells], (1, 0, 2)).reshape(FEAT, 6 * PTS)


def update_source(src_feat, tgt_feat, src_live, tgt_live, lists, target_pot):
    def per_cell(items):
        source_block, source_live, row_cells = items
        pair_cost = pair_costs(source_block, gathered_targets(tgt_feat, row_cells))
        scores = jnp.where(tgt_live[row_cells].reshape(1, -1), (target_pot[row_cells].reshape(1, -1) - pair_cost) / entropy_scale, masked_score)
        peak_score = jnp.max(scores, axis=1)
        totals = jnp.sum(jnp.exp(scores - peak_score[:, None]), axis=1)
        return jnp.where(source_live, -damping * entropy_scale * (peak_score + jnp.log(totals)), 0.0)
    return lax.map(per_cell, (src_feat, src_live, lists))


def update_target(src_feat, tgt_feat, src_live, tgt_live, lists, source_pot):
    def per_cell(items):
        source_block, source_live, source_values, row_cells = items
        pair_cost = pair_costs(source_block, gathered_targets(tgt_feat, row_cells))
        scores = jnp.where(source_live[:, None], (source_values[:, None] - pair_cost) / entropy_scale, masked_score)
        peak_score = jnp.max(scores, axis=0)
        totals = jnp.sum(jnp.exp(scores - peak_score[None, :]), axis=0)
        return peak_score.reshape(6, PTS), totals.reshape(6, PTS)
    peaks, sums = lax.map(per_cell, (src_feat, src_live, source_pot, lists))
    cell_ids = lists.reshape(-1)
    peaks = peaks.reshape(-1, PTS)
    sums = sums.reshape(-1, PTS)
    largest = jnp.full((CELLS, PTS), masked_score, jnp.float32).at[cell_ids].max(peaks)
    totals = jnp.zeros((CELLS, PTS), jnp.float32).at[cell_ids].add(sums * jnp.exp(peaks - largest[cell_ids]))
    return jnp.where(tgt_live, -damping * entropy_scale * (largest + jnp.log(totals)), 0.0)


def reference(src_feat, tgt_feat, src_len, tgt_len, neighbours):
    src_live = live_points(src_len)
    tgt_live = live_points(tgt_len)
    lists = jnp.concatenate([jnp.arange(CELLS, dtype=jnp.int32)[:, None], neighbours.astype(jnp.int32)], axis=1)
    target_pot = jnp.zeros((CELLS, PTS), jnp.float32)
    source_pot = jnp.zeros((CELLS, PTS), jnp.float32)
    for iteration in range(ITERS):
        source_pot = update_source(src_feat, tgt_feat, src_live, tgt_live, lists, target_pot)
        target_pot = update_target(src_feat, tgt_feat, src_live, tgt_live, lists, source_pot)
    return source_pot, target_pot
```

```python
import functools
import math

import jax
import jax.numpy as jnp
from jax import lax
from jax.experimental import pallas as pl
from jax.experimental.pallas import tpu as pltpu
from jax.sharding import PartitionSpec as P

MESH = pl.DeviceIdType.MESH
ITERS = 2
LIST = 6
entropy_scale = 0.5
marginal_weight = 1.0
damping = marginal_weight / (marginal_weight + entropy_scale)
UNIT = math.log2(math.e) / entropy_scale
NEVER = -1.0e30
FAR = 2.0**50
AUX = 16


def peer_of(me, k):
    core, y, z, x = me % 2, (me // 2) % 4, (me // 8) % 4, me // 32
    dcore, dy, dz, dx = k % 2, (k // 2) % 4, (k // 8) % 4, k // 32
    return ((((x + dx) % 4) * 4 + (z + dz) % 4) * 4 + (y + dy) % 4) * 2 + (core + dcore) % 2


def three_parts(value):
    high = value.astype(jnp.bfloat16).astype(jnp.float32)
    rest = value - high
    middle = rest.astype(jnp.bfloat16).astype(jnp.float32)
    return high, middle, rest - middle


def aux_rows(first, value, points):
    row = lax.broadcasted_iota(jnp.int32, (AUX, points), 0)
    rows = jnp.where(row < 6, 1.0, 0.0)
    for i, piece in enumerate(three_parts(value)):
        rows = jnp.where(row == first + i, piece, rows)
    return rows.astype(jnp.bfloat16)


def cross(a, b):
    return lax.dot_general(a, b, (((0,), (0,)), ((), ())), preferred_element_type=jnp.float32)


def kernel(
    n,
    src,
    tgt,
    src_len,
    tgt_len,
    near,
    entry_of,
    asked,
    source_out,
    target_out,
    masked,
    heard,
    row_ids,
    ids,
    send_feat,
    got_feat,
    xaug,
    xnorm,
    yaug,
    ynorm,
    scores,
    part,
    pots,
    send_part,
    got_part,
    send_pot,
    got_pot,
    send_sems,
    recv_sems,
    local_sem,
):
    cells, channels, points = src.shape
    me = lax.axis_index("cells")
    lanes = lax.broadcasted_iota(jnp.int32, (1, points), 1)
    cell_row = lax.broadcasted_iota(jnp.int32, (cells, points), 0)
    top = 3 * channels

    barrier = pltpu.get_barrier_semaphore()

    def greet(k, _):
        pl.semaphore_signal(barrier, inc=1, device_id=(peer_of(me, k),), device_id_type=MESH)
        return 0

    lax.fori_loop(1, n, greet, 0)

    def prepare(c, _):
        live = lanes < tgt_len[c]
        masked[c] = jnp.where(live, tgt[c].astype(jnp.float32), FAR).astype(jnp.bfloat16)
        x = src[c].astype(jnp.float32)
        for i, piece in enumerate(three_parts(x * UNIT)):
            xaug[c, i * channels : (i + 1) * channels] = piece.astype(jnp.bfloat16)
        norm = (-0.5 * UNIT) * jnp.sum(x * x, axis=0, keepdims=True)
        xnorm[c] = norm
        xaug[c, top : top + AUX] = aux_rows(0, norm, points)
        return 0

    lax.fori_loop(0, cells, prepare, 0)
    pl.semaphore_wait(barrier, n - 1)

    def send(outgoing, incoming, sem):
        def go(k, _):
            peer = peer_of(me, k)
            pltpu.make_async_remote_copy(
                src_ref=outgoing.at[peer],
                dst_ref=incoming.at[me],
                send_sem=send_sems.at[sem],
                recv_sem=recv_sems.at[sem],
                device_id=(peer,),
                device_id_type=MESH,
            ).start()
            return 0

        lax.fori_loop(1, n, go, 0)

    def finish(outgoing, incoming, sem):
        every = pltpu.make_async_remote_copy(
            src_ref=outgoing.at[pl.ds(0, n - 1)],
            dst_ref=incoming.at[pl.ds(0, n - 1)],
            send_sem=send_sems.at[sem],
            recv_sem=recv_sems.at[sem],
            device_id=(peer_of(me, 1),),
            device_id_type=MESH,
        )
        every.wait_recv()
        every.wait_send()

    send(asked, heard, 0)
    heard[me] = asked[me]
    finish(asked, heard, 0)
    diagonal = lax.broadcasted_iota(jnp.int32, heard.shape, 0) == lax.broadcasted_iota(
        jnp.int32, heard.shape, 2
    )
    row_ids[...] = jnp.sum(jnp.where(diagonal, heard[...], 0), axis=0)
    to_scalars = pltpu.make_async_copy(row_ids, ids, local_sem)
    to_scalars.start()
    to_scalars.wait()

    def pick_features(p, _):
        send_feat[p] = masked[jnp.maximum(ids[0, p], 0)]
        return 0

    lax.fori_loop(0, n, pick_features, 0)
    send(send_feat, got_feat, 1)

    def place_block(c, k, block):
        columns = slice(k * points, (k + 1) * points)
        for i in range(3):
            yaug[c, i * channels : (i + 1) * channels, columns] = block
        wide = block.astype(jnp.float32)
        norm = (-0.5 * UNIT) * jnp.sum(wide * wide, axis=0, keepdims=True)
        ynorm[c, :, columns] = norm
        yaug[c, top : top + AUX, columns] = aux_rows(3, norm, points)

    def own_block(c, _):
        place_block(c, 0, masked[c])
        return 0

    lax.fori_loop(0, cells, own_block, 0)
    finish(send_feat, got_feat, 1)

    for iteration in range(ITERS):

        def cell(c, carry):
            own, source = carry
            remote = [lax.shift_right_logical(near[c, k], 4) for k in range(LIST - 1)]
            if iteration == 0:
                for k in range(1, LIST):
                    place_block(c, k, got_feat[remote[k - 1]])
            else:
                xaug[c, top : top + AUX] = aux_rows(0, xnorm[c], points)
                for k in range(LIST):
                    columns = slice(k * points, (k + 1) * points)
                    held = pots[c] if k == 0 else got_pot[remote[k - 1]]
                    yaug[c, top : top + AUX, columns] = aux_rows(
                        3, ynorm[c, :, columns] + held, points
                    )
            peak = None
            for k in range(LIST):
                columns = slice(k * points, (k + 1) * points)
                block = cross(yaug[c, :, columns], xaug[c])
                scores[columns] = block
                here = jnp.max(block, axis=0, keepdims=True)
                peak = here if peak is None else jnp.maximum(peak, here)
            total = jnp.zeros((1, points), jnp.float32)
            for k in range(LIST):
                columns = slice(k * points, (k + 1) * points)
                total = total + jnp.sum(jnp.exp2(scores[columns] - peak), axis=0, keepdims=True)
            pot = jnp.where(lanes < src_len[c], -damping * (peak + jnp.log2(total)), 0.0)
            source = jnp.where(cell_row == c, pot, source)
            weight = jnp.where(lanes < src_len[c], pot + xnorm[c], NEVER)
            xaug[c, top : top + AUX] = aux_rows(0, weight, points)
            for k in range(LIST):
                columns = slice(k * points, (k + 1) * points)
                block = cross(xaug[c], yaug[c, :, columns])
                here = jnp.max(block, axis=0, keepdims=True)
                summed = jnp.sum(jnp.exp2(block - here), axis=0, keepdims=True)
                term = here + jnp.log2(summed)
                if iteration > 0:
                    held = pots[c] if k == 0 else got_pot[remote[k - 1]]
                    term = term - held
                if k == 0:
                    own = jnp.where(cell_row == c, term, own)
                else:
                    part[c * (LIST - 1) + k - 1] = term
            return own, source

        nothing = jnp.zeros((cells, points), jnp.float32)
        own, source = lax.fori_loop(0, cells, cell, (nothing, nothing))

        def pick_parts(p, _):
            send_part[iteration, p] = part[entry_of[p]]
            return 0

        lax.fori_loop(0, n, pick_parts, 0)
        send(send_part.at[iteration], got_part.at[iteration], 2 + 2 * iteration)
        if iteration == ITERS - 1:
            source_out[...] = source * (1.0 / UNIT)
        finish(send_part.at[iteration], got_part.at[iteration], 2 + 2 * iteration)

        def larger(p, largest):
            wins = jnp.maximum(largest, got_part[iteration, p])
            return jnp.where(cell_row == ids[0, p], wins, largest)

        largest = lax.fori_loop(0, n, larger, own)

        def add_up(p, totals):
            term = jnp.exp2(got_part[iteration, p] - largest)
            return totals + jnp.where(cell_row == ids[0, p], term, 0.0)

        totals = lax.fori_loop(0, n, add_up, jnp.exp2(own - largest))
        lengths = jnp.zeros((cells, points), jnp.int32)
        for c in range(cells):
            lengths = jnp.where(cell_row == c, tgt_len[c], lengths)
        live = lax.broadcasted_iota(jnp.int32, (cells, points), 1) < lengths
        target = jnp.where(live, -damping * (largest + jnp.log2(totals)), 0.0)
        if iteration == ITERS - 1:
            target_out[...] = target * (1.0 / UNIT)
        else:
            for c in range(cells):
                pots[c] = target[c : c + 1]

            def pick_pots(p, _):
                send_pot[p] = pots[jnp.maximum(ids[0, p], 0)]
                return 0

            lax.fori_loop(0, n, pick_pots, 0)
            send(send_pot, got_pot, 3)
            finish(send_pot, got_pot, 3)


def local(src_feat, tgt_feat, src_len, tgt_len, neighbours):
    cells, channels, points = src_feat.shape
    n = lax.axis_size("cells")
    wanted = neighbours.reshape(-1)
    hits = (wanted // cells)[None, :] == jnp.arange(n, dtype=jnp.int32)[:, None]
    entries = jnp.arange(wanted.shape[0], dtype=jnp.int32)[None, :]
    entry_of = jnp.max(jnp.where(hits, entries, 0), axis=1)
    asked = jnp.max(jnp.where(hits, (wanted % cells)[None, :], -1), axis=1)
    asked = jnp.broadcast_to(asked[:, None, None], (n, 1, 128))
    vmem = pl.BlockSpec(memory_space=pltpu.VMEM)
    smem = pl.BlockSpec(memory_space=pltpu.SMEM)
    deep = 3 * channels + AUX
    f32, bf16 = jnp.float32, jnp.bfloat16
    return pl.pallas_call(
        functools.partial(kernel, n),
        name="sinkhorn",
        out_shape=(jax.ShapeDtypeStruct((cells, points), f32),) * 2,
        in_specs=[vmem, vmem, smem, smem, smem, smem, vmem],
        out_specs=(vmem, vmem),
        scratch_shapes=[
            pltpu.VMEM((cells, channels, points), bf16),
            pltpu.VMEM((n, 1, 128), jnp.int32),
            pltpu.VMEM((1, 128), jnp.int32),
            pltpu.SMEM((1, 128), jnp.int32),
            pltpu.VMEM((n, channels, points), bf16),
            pltpu.VMEM((n, channels, points), bf16),
            pltpu.VMEM((cells, deep, points), bf16),
            pltpu.VMEM((cells, 1, points), f32),
            pltpu.VMEM((cells, deep, LIST * points), bf16),
            pltpu.VMEM((cells, 1, LIST * points), f32),
            pltpu.VMEM((LIST * points, points), f32),
            pltpu.VMEM((cells * (LIST - 1), 1, points), f32),
            pltpu.VMEM((cells, 1, points), f32),
            pltpu.VMEM((ITERS, n, 1, points), f32),
            pltpu.VMEM((ITERS, n, 1, points), f32),
            pltpu.VMEM((n, 1, points), f32),
            pltpu.VMEM((n, 1, points), f32),
            pltpu.SemaphoreType.DMA((5,)),
            pltpu.SemaphoreType.DMA((5,)),
            pltpu.SemaphoreType.DMA(()),
        ],
        compiler_params=pltpu.CompilerParams(
            collective_id=0, has_side_effects=True, vmem_limit_bytes=56 * 2**20
        ),
    )(src_feat, tgt_feat, src_len, tgt_len, neighbours, entry_of, asked)


def solution(mesh):
    split = P("cells")
    return jax.shard_map(
        local,
        mesh=mesh,
        in_specs=(split,) * 5,
        out_specs=(split, split),
        check_vma=False,
    )
```

```python
import functools
import math

import jax
import jax.numpy as jnp
from jax import lax
from jax.experimental import pallas as pl
from jax.experimental.pallas import tpu as pltpu
from jax.sharding import PartitionSpec as P

MESH = pl.DeviceIdType.MESH
ITERS = 2
LIST = 6
entropy_scale = 0.5
marginal_weight = 1.0
damping = marginal_weight / (marginal_weight + entropy_scale)
UNIT = math.log2(math.e) / entropy_scale
NEVER = -1.0e30
FAR = 2.0**50
AUX = 16


def each_peer(me, act):
    core, y = lax.rem(me, 2), lax.rem(lax.div(me, 2), 4)
    z, x = lax.rem(lax.div(me, 8), 4), lax.div(me, 32)
    near = [lax.rem(y + dy, 4) * 2 + lax.rem(core + dc, 2) for dy in range(4) for dc in range(2)]
    for j in range(1, 8):
        act(x * 32 + z * 8 + near[j])

    def plane(i, _):
        k = lax.rem(i * 7, 16)
        base = lax.rem(x + lax.div(k, 4), 4) * 32 + lax.rem(z + lax.rem(k, 4), 4) * 8
        for j in range(8):
            act(base + near[j])
        return 0

    lax.fori_loop(1, 16, plane, 0)


def three_parts(value):
    high = value.astype(jnp.bfloat16).astype(jnp.float32)
    rest = value - high
    middle = rest.astype(jnp.bfloat16).astype(jnp.float32)
    return high, middle, rest - middle


def aux_rows(first, value, points):
    row = lax.broadcasted_iota(jnp.int32, (AUX, points), 0)
    rows = jnp.where(row < 6, 1.0, 0.0)
    for i, piece in enumerate(three_parts(value)):
        rows = jnp.where(row == first + i, piece, rows)
    return rows.astype(jnp.bfloat16)


def cross(a, b):
    return lax.dot_general(a, b, (((0,), (0,)), ((), ())), preferred_element_type=jnp.float32)


def kernel(
    n,
    src,
    tgt,
    src_len,
    tgt_len,
    near,
    entry_of,
    asked,
    source_out,
    target_out,
    masked,
    heard,
    row_ids,
    ids,
    send_feat,
    got_feat,
    xaug,
    xnorm,
    yaug,
    ynorm,
    scores,
    part,
    pots,
    send_part,
    got_part,
    send_pot,
    got_pot,
    send_sems,
    recv_sems,
    local_sem,
):
    cells, channels, points = src.shape
    me = lax.axis_index("cells")
    lanes = lax.broadcasted_iota(jnp.int32, (1, points), 1)
    cell_row = lax.broadcasted_iota(jnp.int32, (cells, points), 0)
    top = 3 * channels

    barrier = pltpu.get_barrier_semaphore()

    def greet(peer):
        pl.semaphore_signal(barrier, inc=1, device_id=(peer,), device_id_type=MESH)

    each_peer(me, greet)

    def prepare(c, _):
        live = lanes < tgt_len[c]
        masked[c] = jnp.where(live, tgt[c].astype(jnp.float32), FAR).astype(jnp.bfloat16)
        x = src[c].astype(jnp.float32)
        for i, piece in enumerate(three_parts(x * UNIT)):
            xaug[c, i * channels : (i + 1) * channels] = piece.astype(jnp.bfloat16)
        norm = (-0.5 * UNIT) * jnp.sum(x * x, axis=0, keepdims=True)
        xnorm[c] = norm
        xaug[c, top : top + AUX] = aux_rows(0, norm, points)
        return 0

    lax.fori_loop(0, cells, prepare, 0)
    pl.semaphore_wait(barrier, n - 1)

    def send(outgoing, incoming, sem):
        def go(peer):
            pltpu.make_async_remote_copy(
                src_ref=outgoing.at[peer],
                dst_ref=incoming.at[me],
                send_sem=send_sems.at[sem],
                recv_sem=recv_sems.at[sem],
                device_id=(peer,),
                device_id_type=MESH,
            ).start()

        each_peer(me, go)

    def finish(outgoing, incoming, sem):
        every = pltpu.make_async_remote_copy(
            src_ref=outgoing.at[pl.ds(0, n - 1)],
            dst_ref=incoming.at[pl.ds(0, n - 1)],
            send_sem=send_sems.at[sem],
            recv_sem=recv_sems.at[sem],
            device_id=(lax.rem(me + 1, n),),
            device_id_type=MESH,
        )
        every.wait_recv()
        every.wait_send()

    send(asked, heard, 0)
    heard[me] = asked[me]
    finish(asked, heard, 0)
    diagonal = lax.broadcasted_iota(jnp.int32, heard.shape, 0) == lax.broadcasted_iota(
        jnp.int32, heard.shape, 2
    )
    row_ids[...] = jnp.sum(jnp.where(diagonal, heard[...], 0), axis=0)
    to_scalars = pltpu.make_async_copy(row_ids, ids, local_sem)
    to_scalars.start()
    to_scalars.wait()

    def pick_features(p, _):
        send_feat[p] = masked[jnp.maximum(ids[0, p], 0)]
        return 0

    lax.fori_loop(0, n, pick_features, 0, unroll=8)
    send(send_feat, got_feat, 1)

    def place_block(c, k, block):
        columns = slice(k * points, (k + 1) * points)
        for i in range(3):
            yaug[c, i * channels : (i + 1) * channels, columns] = block
        wide = block.astype(jnp.float32)
        norm = (-0.5 * UNIT) * jnp.sum(wide * wide, axis=0, keepdims=True)
        ynorm[c, :, columns] = norm
        yaug[c, top : top + AUX, columns] = aux_rows(3, norm, points)

    def own_block(c, _):
        place_block(c, 0, masked[c])
        return 0

    lax.fori_loop(0, cells, own_block, 0)
    finish(send_feat, got_feat, 1)

    for iteration in range(ITERS):

        def cell(c, carry):
            own, source = carry
            remote = [lax.shift_right_logical(near[c, k], 4) for k in range(LIST - 1)]
            if iteration == 0:
                for k in range(1, LIST):
                    place_block(c, k, got_feat[remote[k - 1]])
            else:
                xaug[c, top : top + AUX] = aux_rows(0, xnorm[c], points)
                for k in range(LIST):
                    columns = slice(k * points, (k + 1) * points)
                    held = pots[c] if k == 0 else got_pot[remote[k - 1]]
                    yaug[c, top : top + AUX, columns] = aux_rows(
                        3, ynorm[c, :, columns] + held, points
                    )
            peak = None
            for k in range(LIST):
                columns = slice(k * points, (k + 1) * points)
                block = cross(yaug[c, :, columns], xaug[c])
                scores[columns] = block
                here = jnp.max(block, axis=0, keepdims=True)
                peak = here if peak is None else jnp.maximum(peak, here)
            total = jnp.zeros((1, points), jnp.float32)
            for k in range(LIST):
                columns = slice(k * points, (k + 1) * points)
                total = total + jnp.sum(jnp.exp2(scores[columns] - peak), axis=0, keepdims=True)
            pot = jnp.where(lanes < src_len[c], -damping * (peak + jnp.log2(total)), 0.0)
            source = jnp.where(cell_row == c, pot, source)
            weight = jnp.where(lanes < src_len[c], pot + xnorm[c], NEVER)
            xaug[c, top : top + AUX] = aux_rows(0, weight, points)
            for k in range(LIST):
                columns = slice(k * points, (k + 1) * points)
                block = cross(xaug[c], yaug[c, :, columns])
                here = jnp.max(block, axis=0, keepdims=True)
                summed = jnp.sum(jnp.exp2(block - here), axis=0, keepdims=True)
                term = here + jnp.log2(summed)
                if iteration > 0:
                    held = pots[c] if k == 0 else got_pot[remote[k - 1]]
                    term = term - held
                if k == 0:
                    own = jnp.where(cell_row == c, term, own)
                else:
                    part[c * (LIST - 1) + k - 1] = term
            return own, source

        nothing = jnp.zeros((cells, points), jnp.float32)
        own, source = lax.fori_loop(0, cells, cell, (nothing, nothing))

        def pick_parts(p, _):
            send_part[iteration, p] = part[entry_of[p]]
            return 0

        lax.fori_loop(0, n, pick_parts, 0, unroll=8)
        send(send_part.at[iteration], got_part.at[iteration], 2 + 2 * iteration)
        if iteration == ITERS - 1:
            source_out[...] = source * (1.0 / UNIT)
        finish(send_part.at[iteration], got_part.at[iteration], 2 + 2 * iteration)

        def larger(p, largest):
            wins = jnp.maximum(largest, got_part[iteration, p])
            return jnp.where(cell_row == ids[0, p], wins, largest)

        largest = lax.fori_loop(0, n, larger, own, unroll=8)

        def add_up(p, totals):
            term = jnp.exp2(got_part[iteration, p] - largest)
            return totals + jnp.where(cell_row == ids[0, p], term, 0.0)

        totals = lax.fori_loop(0, n, add_up, jnp.exp2(own - largest), unroll=8)
        lengths = jnp.zeros((cells, points), jnp.int32)
        for c in range(cells):
            lengths = jnp.where(cell_row == c, tgt_len[c], lengths)
        live = lax.broadcasted_iota(jnp.int32, (cells, points), 1) < lengths
        target = jnp.where(live, -damping * (largest + jnp.log2(totals)), 0.0)
        if iteration == ITERS - 1:
            target_out[...] = target * (1.0 / UNIT)
        else:
            for c in range(cells):
                pots[c] = target[c : c + 1]

            def pick_pots(p, _):
                send_pot[p] = pots[jnp.maximum(ids[0, p], 0)]
                return 0

            lax.fori_loop(0, n, pick_pots, 0, unroll=8)
            send(send_pot, got_pot, 3)
            finish(send_pot, got_pot, 3)


def local(src_feat, tgt_feat, src_len, tgt_len, neighbours):
    cells, channels, points = src_feat.shape
    n = lax.axis_size("cells")
    wanted = neighbours.reshape(-1)
    hits = (wanted // cells)[None, :] == jnp.arange(n, dtype=jnp.int32)[:, None]
    entries = jnp.arange(wanted.shape[0], dtype=jnp.int32)[None, :]
    entry_of = jnp.max(jnp.where(hits, entries, 0), axis=1)
    asked = jnp.max(jnp.where(hits, (wanted % cells)[None, :], -1), axis=1)
    asked = jnp.broadcast_to(asked[:, None, None], (n, 1, 128))
    vmem = pl.BlockSpec(memory_space=pltpu.VMEM)
    smem = pl.BlockSpec(memory_space=pltpu.SMEM)
    deep = 3 * channels + AUX
    f32, bf16 = jnp.float32, jnp.bfloat16
    return pl.pallas_call(
        functools.partial(kernel, n),
        name="sinkhorn",
        out_shape=(jax.ShapeDtypeStruct((cells, points), f32),) * 2,
        in_specs=[vmem, vmem, smem, smem, smem, smem, vmem],
        out_specs=(vmem, vmem),
        scratch_shapes=[
            pltpu.VMEM((cells, channels, points), bf16),
            pltpu.VMEM((n, 1, 128), jnp.int32),
            pltpu.VMEM((1, 128), jnp.int32),
            pltpu.SMEM((1, 128), jnp.int32),
            pltpu.VMEM((n, channels, points), bf16),
            pltpu.VMEM((n, channels, points), bf16),
            pltpu.VMEM((cells, deep, points), bf16),
            pltpu.VMEM((cells, 1, points), f32),
            pltpu.VMEM((cells, deep, LIST * points), bf16),
            pltpu.VMEM((cells, 1, LIST * points), f32),
            pltpu.VMEM((LIST * points, points), f32),
            pltpu.VMEM((cells * (LIST - 1), 1, points), f32),
            pltpu.VMEM((cells, 1, points), f32),
            pltpu.VMEM((ITERS, n, 1, points), f32),
            pltpu.VMEM((ITERS, n, 1, points), f32),
            pltpu.VMEM((n, 1, points), f32),
            pltpu.VMEM((n, 1, points), f32),
            pltpu.SemaphoreType.DMA((5,)),
            pltpu.SemaphoreType.DMA((5,)),
            pltpu.SemaphoreType.DMA(()),
        ],
        compiler_params=pltpu.CompilerParams(
            collective_id=0, has_side_effects=True, vmem_limit_bytes=56 * 2**20
        ),
    )(src_feat, tgt_feat, src_len, tgt_len, neighbours, entry_of, asked)


def solution(mesh):
    split = P("cells")
    return jax.shard_map(
        local,
        mesh=mesh,
        in_specs=(split,) * 5,
        out_specs=(split, split),
        check_vma=False,
    )
```

```python
import functools
import math

import jax
import jax.numpy as jnp
from jax import lax
from jax.experimental import pallas as pl
from jax.experimental.pallas import tpu as pltpu
from jax.sharding import PartitionSpec as P

MESH = pl.DeviceIdType.MESH
ITERS = 2
LIST = 6
entropy_scale = 0.5
marginal_weight = 1.0
damping = marginal_weight / (marginal_weight + entropy_scale)
UNIT = math.log2(math.e) / entropy_scale
NEVER = -1.0e30
FAR = 2.0**50
AUX = 16


def coordinates(me):
    return lax.div(me, 32), lax.rem(lax.div(me, 8), 4), lax.rem(lax.div(me, 2), 4), lax.rem(me, 2)


def plane_of(x, z, i, sign):
    k = lax.rem(i * 7, 16)
    dx, dz = lax.div(k, 4), lax.rem(k, 4)
    if sign < 0:
        dx, dz = 4 - dx, 4 - dz
    return lax.rem(x + dx, 4) * 32 + lax.rem(z + dz, 4) * 8


def each_peer(me, act):
    x, z, y, core = coordinates(me)
    near = [lax.rem(y + dy, 4) * 2 + lax.rem(core + dc, 2) for dy in range(4) for dc in range(2)]
    for j in range(1, 8):
        act(x * 32 + z * 8 + near[j], 0)

    def plane(i, _):
        base = plane_of(x, z, i, 1)
        for j in range(8):
            act(base + near[j], i)
        return 0

    lax.fori_loop(1, 16, plane, 0)


def three_parts(value):
    high = value.astype(jnp.bfloat16).astype(jnp.float32)
    rest = value - high
    middle = rest.astype(jnp.bfloat16).astype(jnp.float32)
    return high, middle, rest - middle


def aux_rows(first, value, points):
    row = lax.broadcasted_iota(jnp.int32, (AUX, points), 0)
    rows = jnp.where(row < 6, 1.0, 0.0)
    for i, piece in enumerate(three_parts(value)):
        rows = jnp.where(row == first + i, piece, rows)
    return rows.astype(jnp.bfloat16)


def cross(a, b):
    return lax.dot_general(a, b, (((0,), (0,)), ((), ())), preferred_element_type=jnp.float32)


def column_lse(a, b):
    half = b.shape[1] // 2
    terms = []
    for columns in (slice(0, half), slice(half, 2 * half)):
        block = cross(a, b[:, columns])
        peak = jnp.max(block, axis=0, keepdims=True)
        terms.append(peak + jnp.log2(jnp.sum(jnp.exp2(block - peak), axis=0, keepdims=True)))
    return jnp.concatenate(terms, axis=1)


def kernel(
    n,
    src,
    tgt,
    src_len,
    tgt_len,
    near,
    entry_of,
    asked,
    source_out,
    target_out,
    masked,
    heard,
    row_ids,
    ids,
    send_feat,
    got_feat,
    xaug,
    xnorm,
    yown,
    yown_norm,
    yslot,
    yslot_norm,
    lse_own,
    lse_slot,
    part,
    pots,
    send_part,
    got_part,
    send_pot,
    got_pot,
    send_sems,
    recv_sems,
    feat_sems,
    local_sem,
):
    cells, channels, points = src.shape
    me = lax.axis_index("cells")
    lanes = lax.broadcasted_iota(jnp.int32, (1, points), 1)
    cell_row = lax.broadcasted_iota(jnp.int32, (cells, points), 0)
    top = 3 * channels

    barrier = pltpu.get_barrier_semaphore()

    def greet(peer, _):
        pl.semaphore_signal(barrier, inc=1, device_id=(peer,), device_id_type=MESH)

    each_peer(me, greet)

    def prepare(c, _):
        live = lanes < tgt_len[c]
        masked[c] = jnp.where(live, tgt[c].astype(jnp.float32), FAR).astype(jnp.bfloat16)
        x = src[c].astype(jnp.float32)
        for i, piece in enumerate(three_parts(x * UNIT)):
            xaug[c, i * channels : (i + 1) * channels] = piece.astype(jnp.bfloat16)
        norm = (-0.5 * UNIT) * jnp.sum(x * x, axis=0, keepdims=True)
        xnorm[c] = norm
        xaug[c, top : top + AUX] = aux_rows(0, norm, points)
        return 0

    lax.fori_loop(0, cells, prepare, 0, unroll=2)
    pl.semaphore_wait(barrier, n - 1)

    def send(outgoing, incoming, sem):
        def go(peer, _):
            pltpu.make_async_remote_copy(
                src_ref=outgoing.at[peer],
                dst_ref=incoming.at[me],
                send_sem=send_sems.at[sem],
                recv_sem=recv_sems.at[sem],
                device_id=(peer,),
                device_id_type=MESH,
            ).start()

        each_peer(me, go)

    def arrival(outgoing, incoming, first, count, send_sem, recv_sem):
        return pltpu.make_async_remote_copy(
            src_ref=outgoing.at[pl.ds(0, count)],
            dst_ref=incoming.at[pl.ds(first, count)],
            send_sem=send_sem,
            recv_sem=recv_sem,
            device_id=(lax.rem(me + 1, n),),
            device_id_type=MESH,
        )

    def finish(outgoing, incoming, sem):
        every = arrival(outgoing, incoming, 0, n - 1, send_sems.at[sem], recv_sems.at[sem])
        every.wait_recv()
        every.wait_send()

    send(asked, heard, 0)
    heard[me] = asked[me]
    finish(asked, heard, 0)
    diagonal = lax.broadcasted_iota(jnp.int32, heard.shape, 0) == lax.broadcasted_iota(
        jnp.int32, heard.shape, 2
    )
    row_ids[...] = jnp.sum(jnp.where(diagonal, heard[...], 0), axis=0)
    to_scalars = pltpu.make_async_copy(row_ids, ids, local_sem)
    to_scalars.start()
    to_scalars.wait()

    def pick_features(p, _):
        send_feat[p] = masked[jnp.maximum(ids[0, p], 0)]
        return 0

    lax.fori_loop(0, n, pick_features, 0, unroll=8)

    def send_features(peer, i):
        pltpu.make_async_remote_copy(
            src_ref=send_feat.at[peer],
            dst_ref=got_feat.at[me],
            send_sem=send_sems.at[1],
            recv_sem=feat_sems.at[i],
            device_id=(peer,),
            device_id_type=MESH,
        ).start()

    each_peer(me, send_features)
    got_feat[me] = masked[0]

    def place(block, spread, norms, at):
        for i in range(3):
            spread[at, i * channels : (i + 1) * channels] = block
        wide = block.astype(jnp.float32)
        norm = (-0.5 * UNIT) * jnp.sum(wide * wide, axis=0, keepdims=True)
        norms[at] = norm
        spread[at, top : top + AUX] = aux_rows(3, norm, points)

    def first_own(g, _):
        for j in range(8):
            c = g * 8 + j
            place(masked[c], yown, yown_norm, c)
            lse_own[c] = column_lse(yown[c], xaug[c])
        return 0

    lax.fori_loop(0, cells // 8, first_own, 0)

    x, z, _, _ = coordinates(me)

    def first_slots(i, _):
        base = plane_of(x, z, i, -1)
        arrival(send_feat, got_feat, base, 8, send_sems.at[1], feat_sems.at[i]).wait_recv()
        slots(base)
        return 0

    def slots(base):
        for j in range(8):
            slot = base + j
            place(got_feat[slot], yslot, yslot_norm, slot)
            cell = lax.shift_right_logical(entry_of[slot], 3)
            lse_slot[slot] = column_lse(yslot[slot], xaug[cell])

    home = x * 32 + z * 8
    arrival(send_feat, got_feat, home, 7, send_sems.at[1], feat_sems.at[0]).wait_recv()
    slots(home)
    lax.fori_loop(1, 16, first_slots, 0)
    arrival(send_feat, got_feat, 0, n - 1, send_sems.at[1], feat_sems.at[0]).wait_send()

    def slot_of(c, k):
        return lax.shift_right_logical(near[c, k], 4)

    def stack(rows):
        return jnp.concatenate([rows[c] for c in range(cells)], axis=0)

    for iteration in range(ITERS):
        last = iteration == ITERS - 1

        if iteration > 0:

            def second_rows(g, _):
                for j in range(4):
                    c = g * 4 + j
                    for k in range(LIST - 1):
                        slot = slot_of(c, k)
                        aux = aux_rows(3, yslot_norm[slot] + got_pot[slot], points)
                        block = jnp.concatenate([yslot[slot][:top], aux], axis=0)
                        lse_slot[c * 8 + k] = column_lse(block, xaug[c])
                return 0

            lax.fori_loop(0, cells // 4, second_rows, 0)

        def source_update(c, _):
            if iteration == 0:
                terms = [lse_slot[slot_of(c, k)] for k in range(LIST - 1)] + [lse_own[c]]
            else:
                terms = [lse_slot[c * 8 + k] for k in range(LIST - 1)] + [lse_own[c]]
            peak = functools.reduce(jnp.maximum, terms)
            total = sum(jnp.exp2(term - peak) for term in terms)
            live = lanes < src_len[c]
            pot = jnp.where(live, -damping * (peak + jnp.log2(total)), 0.0)
            if last:
                pots[c] = pot
            xaug[c, top : top + AUX] = aux_rows(0, jnp.where(live, pot + xnorm[c], NEVER), points)
            return 0

        lax.fori_loop(0, cells, source_update, 0, unroll=8)

        def columns(g, _):
            for j in range(4):
                c = g * 4 + j
                for k in range(LIST - 1):
                    part[c * 8 + k] = column_lse(xaug[c], yslot[slot_of(c, k)])
            return 0

        lax.fori_loop(0, cells // 4, columns, 0)

        def pick_parts(p, _):
            send_part[iteration, p] = part[entry_of[p]]
            return 0

        lax.fori_loop(0, n, pick_parts, 0, unroll=8)
        send(send_part.at[iteration], got_part.at[iteration], 2 + 2 * iteration)

        def own_columns(g, _):
            for j in range(8):
                lse_own[g * 8 + j] = column_lse(xaug[g * 8 + j], yown[g * 8 + j])
            return 0

        lax.fori_loop(0, cells // 8, own_columns, 0)
        if last:
            source_out[...] = stack(pots) * (1.0 / UNIT)
        own = stack(lse_own)
        finish(send_part.at[iteration], got_part.at[iteration], 2 + 2 * iteration)

        def larger(p, largest):
            wins = jnp.maximum(largest, got_part[iteration, p])
            return jnp.where(cell_row == ids[0, p], wins, largest)

        largest = lax.fori_loop(0, n, larger, own, unroll=8)

        def add_up(p, totals):
            term = jnp.exp2(got_part[iteration, p] - largest)
            return totals + jnp.where(cell_row == ids[0, p], term, 0.0)

        totals = lax.fori_loop(0, n, add_up, jnp.exp2(own - largest), unroll=8)
        lengths = jnp.zeros((cells, points), jnp.int32)
        for c in range(cells):
            lengths = jnp.where(cell_row == c, tgt_len[c], lengths)
        live = lax.broadcasted_iota(jnp.int32, (cells, points), 1) < lengths
        target = jnp.where(live, -damping * (largest + jnp.log2(totals)), 0.0)
        if last:
            target_out[...] = target * (1.0 / UNIT)
        else:
            for c in range(cells):
                pots[c] = target[c : c + 1]

            def pick_pots(p, _):
                send_pot[p] = pots[jnp.maximum(ids[0, p], 0)]
                return 0

            lax.fori_loop(0, n, pick_pots, 0, unroll=8)
            send(send_pot, got_pot, 3)

            def own_rows(g, _):
                for j in range(8):
                    c = g * 8 + j
                    xaug[c, top : top + AUX] = aux_rows(0, xnorm[c], points)
                    aux = aux_rows(3, yown_norm[c] + pots[c], points)
                    block = jnp.concatenate([yown[c][:top], aux], axis=0)
                    lse_own[c] = column_lse(block, xaug[c])
                return 0

            lax.fori_loop(0, cells // 8, own_rows, 0)
            finish(send_pot, got_pot, 3)


def local(src_feat, tgt_feat, src_len, tgt_len, neighbours):
    cells, channels, points = src_feat.shape
    n = lax.axis_size("cells")
    wanted = neighbours.reshape(-1)
    hits = (wanted // cells)[None, :] == jnp.arange(n, dtype=jnp.int32)[:, None]
    order = jnp.arange(wanted.shape[0], dtype=jnp.int32)[None, :]
    entries = order // 5 * 8 + order % 5
    entry_of = jnp.max(jnp.where(hits, entries, 0), axis=1)
    asked = jnp.max(jnp.where(hits, (wanted % cells)[None, :], -1), axis=1)
    asked = jnp.broadcast_to(asked[:, None, None], (n, 1, 128))
    vmem = pl.BlockSpec(memory_space=pltpu.VMEM)
    smem = pl.BlockSpec(memory_space=pltpu.SMEM)
    deep = 3 * channels + AUX
    f32, bf16 = jnp.float32, jnp.bfloat16
    return pl.pallas_call(
        functools.partial(kernel, n),
        name="sinkhorn",
        out_shape=(jax.ShapeDtypeStruct((cells, points), f32),) * 2,
        in_specs=[vmem, vmem, smem, smem, smem, smem, vmem],
        out_specs=(vmem, vmem),
        scratch_shapes=[
            pltpu.VMEM((cells, channels, points), bf16),
            pltpu.VMEM((n, 1, 128), jnp.int32),
            pltpu.VMEM((1, 128), jnp.int32),
            pltpu.SMEM((1, 128), jnp.int32),
            pltpu.VMEM((n, channels, points), bf16),
            pltpu.VMEM((n, channels, points), bf16),
            pltpu.VMEM((cells, deep, points), bf16),
            pltpu.VMEM((cells, 1, points), f32),
            pltpu.VMEM((cells, deep, points), bf16),
            pltpu.VMEM((cells, 1, points), f32),
            pltpu.VMEM((n, deep, points), bf16),
            pltpu.VMEM((n, 1, points), f32),
            pltpu.VMEM((cells, 1, points), f32),
            pltpu.VMEM((n, 1, points), f32),
            pltpu.VMEM((cells * 8, 1, points), f32),
            pltpu.VMEM((cells, 1, points), f32),
            pltpu.VMEM((ITERS, n, 1, points), f32),
            pltpu.VMEM((ITERS, n, 1, points), f32),
            pltpu.VMEM((n, 1, points), f32),
            pltpu.VMEM((n, 1, points), f32),
            pltpu.SemaphoreType.DMA((5,)),
            pltpu.SemaphoreType.DMA((5,)),
            pltpu.SemaphoreType.DMA((16,)),
            pltpu.SemaphoreType.DMA(()),
        ],
        compiler_params=pltpu.CompilerParams(
            collective_id=0, has_side_effects=True, vmem_limit_bytes=56 * 2**20
        ),
    )(src_feat, tgt_feat, src_len, tgt_len, neighbours, entry_of, asked)


def solution(mesh):
    split = P("cells")
    return jax.shard_map(
        local,
        mesh=mesh,
        in_specs=(split,) * 5,
        out_specs=(split, split),
        check_vma=False,
    )
```

```python
import functools
import math

import jax
import jax.numpy as jnp
from jax import lax
from jax.experimental import pallas as pl
from jax.experimental.pallas import tpu as pltpu
from jax.sharding import PartitionSpec as P

MESH = pl.DeviceIdType.MESH
ITERS = 2
LIST = 6
entropy_scale = 0.5
marginal_weight = 1.0
damping = marginal_weight / (marginal_weight + entropy_scale)
UNIT = math.log2(math.e) / entropy_scale
NEVER = -1.0e30
FAR = 2.0**50
AUX = 16


def coordinates(me):
    return lax.div(me, 32), lax.rem(lax.div(me, 8), 4), lax.rem(lax.div(me, 2), 4), lax.rem(me, 2)


def plane_of(x, z, i, sign, far_first):
    if far_first:
        dx, dz = 6 - lax.div(i, 4), 6 - lax.rem(i, 4)
    else:
        k = lax.rem(i * 7, 16)
        dx, dz = lax.div(k, 4), lax.rem(k, 4)
    if sign < 0:
        dx, dz = 4 - dx, 4 - dz
    return lax.rem(x + dx, 4) * 32 + lax.rem(z + dz, 4) * 8


def each_peer(me, act, far_first=True):
    x, z, y, core = coordinates(me)
    near = [lax.rem(y + dy, 4) * 2 + lax.rem(core + dc, 2) for dy in (2, 1, 3, 0) for dc in range(2)]

    def plane(i, _):
        base = plane_of(x, z, i, 1, far_first)
        for j in range(8):
            act(base + near[j], i)
        return 0

    def home(i):
        for j in (0, 1, 2, 3, 4, 5, 7):
            act(x * 32 + z * 8 + near[j], i)

    if far_first:
        lax.fori_loop(0, 10, plane, 0)
        lax.fori_loop(11, 16, plane, 0)
        home(10)
    else:
        home(0)
        lax.fori_loop(1, 16, plane, 0)


def three_parts(value):
    high = value.astype(jnp.bfloat16).astype(jnp.float32)
    rest = value - high
    middle = rest.astype(jnp.bfloat16).astype(jnp.float32)
    return high, middle, rest - middle


def aux_rows(first, value, points):
    row = lax.broadcasted_iota(jnp.int32, (AUX, points), 0)
    rows = jnp.where(row < 6, 1.0, 0.0)
    for i, piece in enumerate(three_parts(value)):
        rows = jnp.where(row == first + i, piece, rows)
    return rows.astype(jnp.bfloat16)


def cross(a, b):
    return lax.dot_general(a, b, (((0,), (0,)), ((), ())), preferred_element_type=jnp.float32)


def column_lse(a, b):
    half = b.shape[1] // 2
    terms = []
    for columns in (slice(0, half), slice(half, 2 * half)):
        block = cross(a, b[:, columns])
        peak = jnp.max(block, axis=0, keepdims=True)
        terms.append(peak + jnp.log2(jnp.sum(jnp.exp2(block - peak), axis=0, keepdims=True)))
    return jnp.concatenate(terms, axis=1)


def kernel(
    n,
    src,
    tgt,
    src_len,
    tgt_len,
    near,
    source_out,
    target_out,
    masked,
    asked,
    heard,
    row_ids,
    ids,
    held,
    send_feat,
    got_feat,
    xaug,
    xnorm,
    yown,
    yown_norm,
    yslot,
    yslot_norm,
    lse_own,
    lse_slot,
    part,
    pots,
    send_part,
    got_part,
    send_pot,
    got_pot,
    send_sems,
    recv_sems,
    feat_sems,
    local_sem,
):
    cells, channels, points = src.shape
    me = lax.axis_index("cells")
    lanes = lax.broadcasted_iota(jnp.int32, (1, points), 1)
    cell_row = lax.broadcasted_iota(jnp.int32, (cells, points), 0)
    top = 3 * channels

    barrier = pltpu.get_barrier_semaphore()

    def greet(peer, _):
        pl.semaphore_signal(barrier, inc=1, device_id=(peer,), device_id_type=MESH)

    each_peer(me, greet)

    def prepare(c, _):
        live = lanes < tgt_len[c]
        masked[c] = jnp.where(live, tgt[c].astype(jnp.float32), FAR).astype(jnp.bfloat16)
        x = src[c].astype(jnp.float32)
        for i, piece in enumerate(three_parts(x * UNIT)):
            xaug[c, i * channels : (i + 1) * channels] = piece.astype(jnp.bfloat16)
        norm = (-0.5 * UNIT) * jnp.sum(x * x, axis=0, keepdims=True)
        xnorm[c] = norm
        xaug[c, top : top + AUX] = aux_rows(0, norm, points)
        return 0

    lax.fori_loop(0, cells, prepare, 0, unroll=2)

    device_row = lax.broadcasted_iota(jnp.int32, (n, 128), 0)
    on_diagonal = device_row == lax.broadcasted_iota(jnp.int32, (n, 128), 1)

    def ask(c, table):
        for k in range(LIST - 1):
            wanted = near[k, c]
            entry = (c * 8 + k) * 16 + jnp.bitwise_and(wanted, 15)
            table = jnp.where(device_row == lax.shift_right_logical(wanted, 4), entry, table)
        return table

    table = lax.fori_loop(0, cells, ask, jnp.full((n, 128), -1, jnp.int32))
    asked[...] = table.reshape(n, 1, 128)

    def to_scalars(diagonal_of, at):
        row_ids[at] = jnp.sum(jnp.where(on_diagonal, diagonal_of, 0), axis=0, keepdims=True)
        copy = pltpu.make_async_copy(row_ids.at[at], ids.at[at], local_sem)
        copy.start()
        copy.wait()

    to_scalars(table, 0)
    pl.semaphore_wait(barrier, n - 1)

    def send(outgoing, incoming, sem):
        def go(peer, _):
            pltpu.make_async_remote_copy(
                src_ref=outgoing.at[peer],
                dst_ref=incoming.at[me],
                send_sem=send_sems.at[sem],
                recv_sem=recv_sems.at[sem],
                device_id=(peer,),
                device_id_type=MESH,
            ).start()

        each_peer(me, go)

    def arrival(outgoing, incoming, first, count, send_sem, recv_sem):
        return pltpu.make_async_remote_copy(
            src_ref=outgoing.at[pl.ds(0, count)],
            dst_ref=incoming.at[pl.ds(first, count)],
            send_sem=send_sem,
            recv_sem=recv_sem,
            device_id=(lax.rem(me + 1, n),),
            device_id_type=MESH,
        )

    def finish(outgoing, incoming, sem):
        every = arrival(outgoing, incoming, 0, n - 1, send_sems.at[sem], recv_sems.at[sem])
        every.wait_recv()
        every.wait_send()

    send(asked, heard, 0)
    heard[me] = asked[me]
    finish(asked, heard, 0)
    to_scalars(heard[...].reshape(n, 128), 1)

    def entry_of(p):
        return lax.shift_right_logical(jnp.maximum(ids[0, 0, p], 0), 4)

    def cell_for(p):
        return jnp.bitwise_and(ids[1, 0, p], 15)

    def row_for(p):
        return jnp.where(ids[1, 0, p] < 0, -1, cell_for(p))

    def pick_features(p, _):
        send_feat[p] = masked[cell_for(p)]
        return 0

    lax.fori_loop(0, n, pick_features, 0, unroll=8)

    def send_features(peer, i):
        pltpu.make_async_remote_copy(
            src_ref=send_feat.at[peer],
            dst_ref=got_feat.at[me],
            send_sem=send_sems.at[1],
            recv_sem=feat_sems.at[i],
            device_id=(peer,),
            device_id_type=MESH,
        ).start()

    each_peer(me, send_features, False)
    got_feat[me] = masked[0]

    def place(block, spread, norms, at):
        for i in range(3):
            spread[at, i * channels : (i + 1) * channels] = block
        wide = block.astype(jnp.float32)
        norm = (-0.5 * UNIT) * jnp.sum(wide * wide, axis=0, keepdims=True)
        norms[at] = norm
        spread[at, top : top + AUX] = aux_rows(3, norm, points)

    def first_own(g, _):
        for j in range(8):
            c = g * 8 + j
            place(masked[c], yown, yown_norm, c)
            lse_own[c] = column_lse(yown[c], xaug[c])
        return 0

    lax.fori_loop(0, cells // 8, first_own, 0)

    x, z, _, _ = coordinates(me)

    def first_slots(i, _):
        base = plane_of(x, z, i, -1, False)
        arrival(send_feat, got_feat, base, 8, send_sems.at[1], feat_sems.at[i]).wait_recv()
        slots(base)
        return 0

    def slots(base):
        for j in range(8):
            slot = base + j
            place(got_feat[slot], yslot, yslot_norm, slot)
            cell = lax.shift_right_logical(entry_of(slot), 3)
            lse_slot[slot] = column_lse(yslot[slot], xaug[cell])

    home = x * 32 + z * 8
    arrival(send_feat, got_feat, home, 7, send_sems.at[1], feat_sems.at[0]).wait_recv()
    slots(home)
    lax.fori_loop(1, 16, first_slots, 0)
    arrival(send_feat, got_feat, 0, n - 1, send_sems.at[1], feat_sems.at[0]).wait_send()

    def slot_of(c, k):
        return lax.shift_right_logical(near[k, c], 4)

    def stack(rows):
        return jnp.concatenate([rows[c] for c in range(cells)], axis=0)

    for iteration in range(ITERS):
        last = iteration == ITERS - 1

        if iteration > 0:

            def second_rows(g, _):
                for j in range(4):
                    c = g * 4 + j
                    for k in range(LIST - 1):
                        slot = slot_of(c, k)
                        aux = aux_rows(3, yslot_norm[slot] + got_pot[slot], points)
                        block = jnp.concatenate([yslot[slot][:top], aux], axis=0)
                        lse_slot[c * 8 + k] = column_lse(block, xaug[c])
                return 0

            lax.fori_loop(0, cells // 4, second_rows, 0)

        def source_update(c, _):
            if iteration == 0:
                terms = [lse_slot[slot_of(c, k)] for k in range(LIST - 1)] + [lse_own[c]]
            else:
                terms = [lse_slot[c * 8 + k] for k in range(LIST - 1)] + [lse_own[c]]
            peak = functools.reduce(jnp.maximum, terms)
            total = sum(jnp.exp2(term - peak) for term in terms)
            live = lanes < src_len[c]
            pot = jnp.where(live, -damping * (peak + jnp.log2(total)), 0.0)
            if last:
                pots[c] = pot
            xaug[c, top : top + AUX] = aux_rows(0, jnp.where(live, pot + xnorm[c], NEVER), points)
            return 0

        lax.fori_loop(0, cells, source_update, 0, unroll=8)

        def columns(g, _):
            for j in range(4):
                c = g * 4 + j
                for k in range(LIST - 1):
                    part[c * 8 + k] = column_lse(xaug[c], yslot[slot_of(c, k)])
            return 0

        lax.fori_loop(0, cells // 4, columns, 0)

        def pick_parts(p, _):
            send_part[iteration, p] = part[entry_of(p)]
            return 0

        lax.fori_loop(0, n, pick_parts, 0, unroll=8)
        send(send_part.at[iteration], got_part.at[iteration], 2 + 2 * iteration)

        def own_columns(g, _):
            for j in range(8):
                lse_own[g * 8 + j] = column_lse(xaug[g * 8 + j], yown[g * 8 + j])
            return 0

        lax.fori_loop(0, cells // 8, own_columns, 0)
        if last:
            source_out[...] = stack(pots)
        own = stack(lse_own)
        finish(send_part.at[iteration], got_part.at[iteration], 2 + 2 * iteration)

        def larger(p, largest):
            wins = jnp.maximum(largest, got_part[iteration, p])
            return jnp.where(cell_row == row_for(p), wins, largest)

        largest = lax.fori_loop(0, n, larger, own, unroll=8)

        for c in range(cells):
            held[c] = largest[c : c + 1]

        def add_up(p, totals):
            term = jnp.exp2(got_part[iteration, p] - held[cell_for(p)])
            return totals + jnp.where(cell_row == row_for(p), term, 0.0)

        totals = lax.fori_loop(0, n, add_up, jnp.exp2(own - largest), unroll=8)
        lengths = jnp.zeros((cells, points), jnp.int32)
        for c in range(cells):
            lengths = jnp.where(cell_row == c, tgt_len[c], lengths)
        live = lax.broadcasted_iota(jnp.int32, (cells, points), 1) < lengths
        target = jnp.where(live, -damping * (largest + jnp.log2(totals)), 0.0)
        if last:
            target_out[...] = target
        else:
            for c in range(cells):
                pots[c] = target[c : c + 1]

            def pick_pots(p, _):
                send_pot[p] = pots[cell_for(p)]
                return 0

            lax.fori_loop(0, n, pick_pots, 0, unroll=8)
            send(send_pot, got_pot, 3)

            def own_rows(g, _):
                for j in range(8):
                    c = g * 8 + j
                    xaug[c, top : top + AUX] = aux_rows(0, xnorm[c], points)
                    aux = aux_rows(3, yown_norm[c] + pots[c], points)
                    block = jnp.concatenate([yown[c][:top], aux], axis=0)
                    lse_own[c] = column_lse(block, xaug[c])
                return 0

            lax.fori_loop(0, cells // 8, own_rows, 0)
            finish(send_pot, got_pot, 3)


def local(src_feat, tgt_feat, src_len, tgt_len, neighbours):
    cells, channels, points = src_feat.shape
    n = lax.axis_size("cells")
    vmem = pl.BlockSpec(memory_space=pltpu.VMEM)
    smem = pl.BlockSpec(memory_space=pltpu.SMEM)
    deep = 3 * channels + AUX
    f32, bf16 = jnp.float32, jnp.bfloat16
    potentials = pl.pallas_call(
        functools.partial(kernel, n),
        name="sinkhorn",
        out_shape=(jax.ShapeDtypeStruct((cells, points), f32),) * 2,
        in_specs=[vmem, vmem, smem, smem, smem],
        out_specs=(vmem, vmem),
        scratch_shapes=[
            pltpu.VMEM((cells, channels, points), bf16),
            pltpu.VMEM((n, 1, 128), jnp.int32),
            pltpu.VMEM((n, 1, 128), jnp.int32),
            pltpu.VMEM((2, 1, 128), jnp.int32),
            pltpu.SMEM((2, 1, 128), jnp.int32),
            pltpu.VMEM((cells, 1, points), f32),
            pltpu.VMEM((n, channels, points), bf16),
            pltpu.VMEM((n, channels, points), bf16),
            pltpu.VMEM((cells, deep, points), bf16),
            pltpu.VMEM((cells, 1, points), f32),
            pltpu.VMEM((cells, deep, points), bf16),
            pltpu.VMEM((cells, 1, points), f32),
            pltpu.VMEM((n, deep, points), bf16),
            pltpu.VMEM((n, 1, points), f32),
            pltpu.VMEM((cells, 1, points), f32),
            pltpu.VMEM((n, 1, points), f32),
            pltpu.VMEM((cells * 8, 1, points), f32),
            pltpu.VMEM((cells, 1, points), f32),
            pltpu.VMEM((ITERS, n, 1, points), f32),
            pltpu.VMEM((ITERS, n, 1, points), f32),
            pltpu.VMEM((n, 1, points), f32),
            pltpu.VMEM((n, 1, points), f32),
            pltpu.SemaphoreType.DMA((5,)),
            pltpu.SemaphoreType.DMA((5,)),
            pltpu.SemaphoreType.DMA((16,)),
            pltpu.SemaphoreType.DMA(()),
        ],
        compiler_params=pltpu.CompilerParams(
            collective_id=0, has_side_effects=True, vmem_limit_bytes=56 * 2**20
        ),
    )(src_feat, tgt_feat, src_len, tgt_len, neighbours.T)
    return tuple(potential * (1.0 / UNIT) for potential in potentials)


def solution(mesh):
    split = P("cells")
    return jax.shard_map(
        local,
        mesh=mesh,
        in_specs=(split,) * 5,
        out_specs=(split, split),
        check_vma=False,
    )
```

```python
import functools
import math

import jax
import jax.numpy as jnp
from jax import lax
from jax.experimental import pallas as pl
from jax.experimental.pallas import tpu as pltpu
from jax.sharding import PartitionSpec as P

MESH = pl.DeviceIdType.MESH
ITERS = 2
LIST = 6
entropy_scale = 0.5
marginal_weight = 1.0
damping = marginal_weight / (marginal_weight + entropy_scale)
UNIT = math.log2(math.e) / entropy_scale
NEVER = -1.0e30
LOWEST = -3.0e38
FAR = 2.0**50
AUX = 16


def coordinates(me):
    return lax.div(me, 32), lax.rem(lax.div(me, 8), 4), lax.rem(lax.div(me, 2), 4), lax.rem(me, 2)


def plane_of(x, z, i, sign, far_first):
    if far_first:
        dx, dz = 6 - lax.div(i, 4), 6 - lax.rem(i, 4)
    else:
        k = lax.rem(i * 7, 16)
        dx, dz = lax.div(k, 4), lax.rem(k, 4)
    if sign < 0:
        dx, dz = 4 - dx, 4 - dz
    return lax.rem(x + dx, 4) * 32 + lax.rem(z + dz, 4) * 8


def each_peer(me, act, far_first=True):
    x, z, y, core = coordinates(me)
    near = [lax.rem(y + dy, 4) * 2 + lax.rem(core + dc, 2) for dy in (2, 1, 3, 0) for dc in range(2)]

    def plane(i, _):
        base = plane_of(x, z, i, 1, far_first)
        for j in range(8):
            act(base + near[j], i)
        return 0

    def home(i):
        for j in (0, 1, 2, 3, 4, 5, 7):
            act(x * 32 + z * 8 + near[j], i)

    if far_first:
        lax.fori_loop(0, 10, plane, 0)
        lax.fori_loop(11, 16, plane, 0)
        home(10)
    else:
        home(0)
        lax.fori_loop(1, 16, plane, 0)


def three_parts(value):
    high = value.astype(jnp.bfloat16).astype(jnp.float32)
    rest = value - high
    middle = rest.astype(jnp.bfloat16).astype(jnp.float32)
    return high, middle, rest - middle


def aux_rows(first, value, points):
    row = lax.broadcasted_iota(jnp.int32, (AUX, points), 0)
    rows = jnp.where(row < 6, 1.0, 0.0)
    for i, piece in enumerate(three_parts(value)):
        rows = jnp.where(row == first + i, piece, rows)
    return rows.astype(jnp.bfloat16)


def cross(a, b):
    return lax.dot_general(a, b, (((0,), (0,)), ((), ())), preferred_element_type=jnp.float32)


def column_lse(a, b):
    half = b.shape[1] // 2
    terms = []
    for columns in (slice(0, half), slice(half, 2 * half)):
        block = cross(a, b[:, columns])
        peak = jnp.max(block, axis=0, keepdims=True)
        terms.append(peak + jnp.log2(jnp.sum(jnp.exp2(block - peak), axis=0, keepdims=True)))
    return jnp.concatenate(terms, axis=1)


def kernel(
    n,
    src,
    tgt,
    src_len,
    tgt_len,
    near,
    source_out,
    target_out,
    masked,
    asked,
    heard,
    row_ids,
    ids,
    send_feat,
    got_feat,
    xaug,
    xnorm,
    yown,
    yown_norm,
    yslot,
    yslot_norm,
    lse_own,
    lse_slot,
    part,
    pots,
    send_part,
    got_part,
    send_pot,
    got_pot,
    send_sems,
    recv_sems,
    feat_sems,
    local_sem,
):
    cells, channels, points = src.shape
    me = lax.axis_index("cells")
    lanes = lax.broadcasted_iota(jnp.int32, (1, points), 1)
    cell_row = lax.broadcasted_iota(jnp.int32, (cells, points), 0)
    top = 3 * channels

    barrier = pltpu.get_barrier_semaphore()

    def greet(peer, _):
        pl.semaphore_signal(barrier, inc=1, device_id=(peer,), device_id_type=MESH)

    each_peer(me, greet)

    def prepare(c, _):
        live = lanes < tgt_len[c]
        masked[c] = jnp.where(live, tgt[c].astype(jnp.float32), FAR).astype(jnp.bfloat16)
        x = src[c].astype(jnp.float32)
        for i, piece in enumerate(three_parts(x * UNIT)):
            xaug[c, i * channels : (i + 1) * channels] = piece.astype(jnp.bfloat16)
        norm = (-0.5 * UNIT) * jnp.sum(x * x, axis=0, keepdims=True)
        xnorm[c] = norm
        xaug[c, top : top + AUX] = aux_rows(0, norm, points)
        return 0


    device_row = lax.broadcasted_iota(jnp.int32, (n, 128), 0)
    on_diagonal = device_row == lax.broadcasted_iota(jnp.int32, (n, 128), 1)

    def ask(c, table):
        for k in range(LIST - 1):
            wanted = near[k, c]
            entry = (c * 8 + k) * 16 + jnp.bitwise_and(wanted, 15)
            table = jnp.where(device_row == lax.shift_right_logical(wanted, 4), entry, table)
        return table

    table = lax.fori_loop(0, cells, ask, jnp.full((n, 128), -1, jnp.int32))
    asked[...] = table.reshape(n, 1, 128)

    def to_scalars(diagonal_of, at):
        row_ids[at] = jnp.sum(jnp.where(on_diagonal, diagonal_of, 0), axis=0, keepdims=True)
        copy = pltpu.make_async_copy(row_ids.at[at], ids.at[at], local_sem)
        copy.start()
        copy.wait()

    pl.semaphore_wait(barrier, n - 1)

    def send(outgoing, incoming, sem):
        def go(peer, _):
            pltpu.make_async_remote_copy(
                src_ref=outgoing.at[peer],
                dst_ref=incoming.at[me],
                send_sem=send_sems.at[sem],
                recv_sem=recv_sems.at[sem],
                device_id=(peer,),
                device_id_type=MESH,
            ).start()

        each_peer(me, go)

    def arrival(outgoing, incoming, first, count, send_sem, recv_sem):
        return pltpu.make_async_remote_copy(
            src_ref=outgoing.at[pl.ds(0, count)],
            dst_ref=incoming.at[pl.ds(first, count)],
            send_sem=send_sem,
            recv_sem=recv_sem,
            device_id=(lax.rem(me + 1, n),),
            device_id_type=MESH,
        )

    def finish(outgoing, incoming, sem):
        every = arrival(outgoing, incoming, 0, n - 1, send_sems.at[sem], recv_sems.at[sem])
        every.wait_recv()
        every.wait_send()

    send(asked, heard, 0)
    lax.fori_loop(0, cells, prepare, 0, unroll=2)
    to_scalars(table, 0)
    heard[me] = asked[me]
    finish(asked, heard, 0)
    to_scalars(heard[...].reshape(n, 128), 1)

    def entry_of(p):
        return lax.shift_right_logical(jnp.maximum(ids[0, 0, p], 0), 4)

    def cell_for(p):
        return jnp.bitwise_and(ids[1, 0, p], 15)

    packed = heard[...].reshape(n, 128)
    asker_cell = jnp.where(packed < 0, -1, jnp.bitwise_and(packed, 15))
    lane_of = lax.broadcasted_iota(jnp.int32, (n, 128), 1)
    to_cell = jnp.where(asker_cell == lane_of, 1.0, 0.0).astype(jnp.bfloat16)
    in_parts = jnp.logical_and(asker_cell == jnp.bitwise_and(lane_of, 15), lane_of < 3 * cells)
    from_parts = jnp.where(in_parts, 1.0, 0.0).astype(jnp.bfloat16)

    def for_askers(rows):
        parts = list(three_parts(rows)) + [jnp.zeros((128 - 3 * cells, points), jnp.float32)]
        stacked = jnp.concatenate(parts, axis=0).astype(jnp.bfloat16)
        return jnp.dot(from_parts, stacked, preferred_element_type=jnp.float32)

    def pick_features(p, _):
        send_feat[p] = masked[cell_for(p)]
        return 0

    lax.fori_loop(0, n, pick_features, 0, unroll=8)

    def send_features(peer, i):
        pltpu.make_async_remote_copy(
            src_ref=send_feat.at[peer],
            dst_ref=got_feat.at[me],
            send_sem=send_sems.at[1],
            recv_sem=feat_sems.at[i],
            device_id=(peer,),
            device_id_type=MESH,
        ).start()

    each_peer(me, send_features, False)
    got_feat[me] = masked[0]

    def place(block, spread, norms, at):
        for i in range(3):
            spread[at, i * channels : (i + 1) * channels] = block
        wide = block.astype(jnp.float32)
        norm = (-0.5 * UNIT) * jnp.sum(wide * wide, axis=0, keepdims=True)
        norms[at] = norm
        spread[at, top : top + AUX] = aux_rows(3, norm, points)

    def first_own(g, _):
        for j in range(8):
            c = g * 8 + j
            place(masked[c], yown, yown_norm, c)
            lse_own[c] = column_lse(yown[c], xaug[c])
        return 0

    lax.fori_loop(0, cells // 8, first_own, 0)

    x, z, _, _ = coordinates(me)

    def first_slots(i, _):
        base = plane_of(x, z, i, -1, False)
        arrival(send_feat, got_feat, base, 8, send_sems.at[1], feat_sems.at[i]).wait_recv()
        slots(base)
        return 0

    def slots(base):
        for j in range(8):
            slot = base + j
            place(got_feat[slot], yslot, yslot_norm, slot)
            cell = lax.shift_right_logical(entry_of(slot), 3)
            lse_slot[slot] = column_lse(yslot[slot], xaug[cell])

    home = x * 32 + z * 8
    arrival(send_feat, got_feat, home, 7, send_sems.at[1], feat_sems.at[0]).wait_recv()
    slots(home)
    lax.fori_loop(1, 16, first_slots, 0)
    arrival(send_feat, got_feat, 0, n - 1, send_sems.at[1], feat_sems.at[0]).wait_send()

    def slot_of(c, k):
        return lax.shift_right_logical(near[k, c], 4)

    def stack(rows):
        return jnp.concatenate([rows[c] for c in range(cells)], axis=0)

    for iteration in range(ITERS):
        last = iteration == ITERS - 1

        if iteration > 0:

            def second_rows(g, _):
                for j in range(8):
                    c = g * 8 + j
                    for k in range(LIST - 1):
                        slot = slot_of(c, k)
                        aux = aux_rows(3, yslot_norm[slot] + got_pot[slot], points)
                        block = jnp.concatenate([yslot[slot][:top], aux], axis=0)
                        lse_slot[c * 8 + k] = column_lse(block, xaug[c])
                return 0

            lax.fori_loop(0, cells // 8, second_rows, 0)

        def source_update(c, _):
            if iteration == 0:
                terms = [lse_slot[slot_of(c, k)] for k in range(LIST - 1)] + [lse_own[c]]
            else:
                terms = [lse_slot[c * 8 + k] for k in range(LIST - 1)] + [lse_own[c]]
            peak = functools.reduce(jnp.maximum, terms)
            total = sum(jnp.exp2(term - peak) for term in terms)
            live = lanes < src_len[c]
            pot = jnp.where(live, -damping * (peak + jnp.log2(total)), 0.0)
            if last:
                pots[c] = pot
            xaug[c, top : top + AUX] = aux_rows(0, jnp.where(live, pot + xnorm[c], NEVER), points)
            return 0

        lax.fori_loop(0, cells, source_update, 0, unroll=8)

        def columns(g, _):
            for j in range(8):
                c = g * 8 + j
                for k in range(LIST - 1):
                    part[c * 8 + k] = column_lse(xaug[c], yslot[slot_of(c, k)])
            return 0

        lax.fori_loop(0, cells // 8, columns, 0)

        def pick_parts(p, _):
            send_part[iteration, p] = part[entry_of(p)]
            return 0

        lax.fori_loop(0, n, pick_parts, 0, unroll=8)
        send(send_part.at[iteration], got_part.at[iteration], 2 + 2 * iteration)

        def own_columns(g, _):
            for j in range(8):
                lse_own[g * 8 + j] = column_lse(xaug[g * 8 + j], yown[g * 8 + j])
            return 0

        lax.fori_loop(0, cells // 8, own_columns, 0)
        if last:
            source_out[...] = stack(pots)
        own = stack(lse_own)
        finish(send_part.at[iteration], got_part.at[iteration], 2 + 2 * iteration)

        terms = got_part[iteration].reshape(n, points)
        asker = jnp.concatenate([asker_cell] * (points // 128), axis=1)
        best = [
            jnp.max(jnp.where(asker == c, terms, LOWEST), axis=0, keepdims=True)
            for c in range(cells)
        ]
        largest = jnp.maximum(own, jnp.concatenate(best, axis=0))
        shifted = jnp.where(asker >= 0, jnp.exp2(terms - for_askers(largest)), 0.0)
        arrived = sum(cross(to_cell, piece.astype(jnp.bfloat16)) for piece in three_parts(shifted))
        totals = jnp.exp2(own - largest) + arrived[:cells]
        lengths = jnp.zeros((cells, points), jnp.int32)
        for c in range(cells):
            lengths = jnp.where(cell_row == c, tgt_len[c], lengths)
        live = lax.broadcasted_iota(jnp.int32, (cells, points), 1) < lengths
        target = jnp.where(live, -damping * (largest + jnp.log2(totals)), 0.0)
        if last:
            target_out[...] = target
        else:
            for c in range(cells):
                pots[c] = target[c : c + 1]
            send_pot[...] = for_askers(target).reshape(n, 1, points)
            send(send_pot, got_pot, 3)

            def own_rows(g, _):
                for j in range(8):
                    c = g * 8 + j
                    xaug[c, top : top + AUX] = aux_rows(0, xnorm[c], points)
                    aux = aux_rows(3, yown_norm[c] + pots[c], points)
                    block = jnp.concatenate([yown[c][:top], aux], axis=0)
                    lse_own[c] = column_lse(block, xaug[c])
                return 0

            lax.fori_loop(0, cells // 8, own_rows, 0)
            finish(send_pot, got_pot, 3)


def local(src_feat, tgt_feat, src_len, tgt_len, neighbours):
    cells, channels, points = src_feat.shape
    n = lax.axis_size("cells")
    vmem = pl.BlockSpec(memory_space=pltpu.VMEM)
    smem = pl.BlockSpec(memory_space=pltpu.SMEM)
    deep = 3 * channels + AUX
    f32, bf16 = jnp.float32, jnp.bfloat16
    potentials = pl.pallas_call(
        functools.partial(kernel, n),
        name="sinkhorn",
        out_shape=(jax.ShapeDtypeStruct((cells, points), f32),) * 2,
        in_specs=[vmem, vmem, smem, smem, smem],
        out_specs=(vmem, vmem),
        scratch_shapes=[
            pltpu.VMEM((cells, channels, points), bf16),
            pltpu.VMEM((n, 1, 128), jnp.int32),
            pltpu.VMEM((n, 1, 128), jnp.int32),
            pltpu.VMEM((2, 1, 128), jnp.int32),
            pltpu.SMEM((2, 1, 128), jnp.int32),
            pltpu.VMEM((n, channels, points), bf16),
            pltpu.VMEM((n, channels, points), bf16),
            pltpu.VMEM((cells, deep, points), bf16),
            pltpu.VMEM((cells, 1, points), f32),
            pltpu.VMEM((cells, deep, points), bf16),
            pltpu.VMEM((cells, 1, points), f32),
            pltpu.VMEM((n, deep, points), bf16),
            pltpu.VMEM((n, 1, points), f32),
            pltpu.VMEM((cells, 1, points), f32),
            pltpu.VMEM((n, 1, points), f32),
            pltpu.VMEM((cells * 8, 1, points), f32),
            pltpu.VMEM((cells, 1, points), f32),
            pltpu.VMEM((ITERS, n, 1, points), f32),
            pltpu.VMEM((ITERS, n, 1, points), f32),
            pltpu.VMEM((n, 1, points), f32),
            pltpu.VMEM((n, 1, points), f32),
            pltpu.SemaphoreType.DMA((5,)),
            pltpu.SemaphoreType.DMA((5,)),
            pltpu.SemaphoreType.DMA((16,)),
            pltpu.SemaphoreType.DMA(()),
        ],
        compiler_params=pltpu.CompilerParams(
            collective_id=0, has_side_effects=True, vmem_limit_bytes=56 * 2**20
        ),
    )(src_feat, tgt_feat, src_len, tgt_len, neighbours.T)
    return tuple(potential * (1.0 / UNIT) for potential in potentials)


def solution(mesh):
    split = P("cells")
    return jax.shard_map(
        local,
        mesh=mesh,
        in_specs=(split,) * 5,
        out_specs=(split, split),
        check_vma=False,
    )
```

```python
import functools
import math

import jax
import jax.numpy as jnp
from jax import lax
from jax.experimental import pallas as pl
from jax.experimental.pallas import tpu as pltpu
from jax.sharding import PartitionSpec as P

MESH = pl.DeviceIdType.MESH
ITERS = 2
LIST = 6
entropy_scale = 0.5
marginal_weight = 1.0
damping = marginal_weight / (marginal_weight + entropy_scale)
UNIT = math.log2(math.e) / entropy_scale
NEVER = -1.0e30
LOWEST = -3.0e38
FAR = 2.0**50
AUX = 16


def coordinates(me):
    return lax.div(me, 32), lax.rem(lax.div(me, 8), 4), lax.rem(lax.div(me, 2), 4), lax.rem(me, 2)


def plane_of(x, z, i, sign, far_first):
    if far_first:
        dx, dz = 6 - lax.div(i, 4), 6 - lax.rem(i, 4)
    else:
        k = lax.rem(i * 7, 16)
        dx, dz = lax.div(k, 4), lax.rem(k, 4)
    if sign < 0:
        dx, dz = 4 - dx, 4 - dz
    return lax.rem(x + dx, 4) * 32 + lax.rem(z + dz, 4) * 8


def each_peer(me, act, far_first=True):
    x, z, y, core = coordinates(me)
    near = [lax.rem(y + dy, 4) * 2 + lax.rem(core + dc, 2) for dy in (2, 1, 3, 0) for dc in range(2)]

    def plane(i, _):
        base = plane_of(x, z, i, 1, far_first)
        for j in range(8):
            act(base + near[j], i)
        return 0

    def home(i):
        for j in (0, 1, 2, 3, 4, 5, 7):
            act(x * 32 + z * 8 + near[j], i)

    if far_first:
        lax.fori_loop(0, 10, plane, 0)
        lax.fori_loop(11, 16, plane, 0)
        home(10)
    else:
        home(0)
        lax.fori_loop(1, 16, plane, 0)


def three_parts(value):
    high = value.astype(jnp.bfloat16).astype(jnp.float32)
    rest = value - high
    middle = rest.astype(jnp.bfloat16).astype(jnp.float32)
    return high, middle, rest - middle


def aux_rows(first, value, points):
    row = lax.broadcasted_iota(jnp.int32, (AUX, points), 0)
    rows = jnp.where(row < 6, 1.0, 0.0)
    for i, piece in enumerate(three_parts(value)):
        rows = jnp.where(row == first + i, piece, rows)
    return rows.astype(jnp.bfloat16)


def cross(a, b):
    return lax.dot_general(a, b, (((0,), (0,)), ((), ())), preferred_element_type=jnp.float32)


def column_lse(a, b):
    half = b.shape[1] // 2
    terms = []
    for columns in (slice(0, half), slice(half, 2 * half)):
        block = cross(a, b[:, columns])
        peak = jnp.max(block, axis=0, keepdims=True)
        terms.append(peak + jnp.log2(jnp.sum(jnp.exp2(block - peak), axis=0, keepdims=True)))
    return jnp.concatenate(terms, axis=1)


def kernel(
    n,
    src,
    tgt,
    src_len,
    tgt_len,
    near,
    source_out,
    target_out,
    masked,
    asked,
    heard,
    row_ids,
    ids,
    send_feat,
    got_feat,
    xaug,
    xnorm,
    yown,
    yown_norm,
    yslot,
    yslot_norm,
    lse_own,
    lse_slot,
    part,
    pots,
    send_part,
    got_part,
    send_pot,
    got_pot,
    send_sems,
    recv_sems,
    feat_sems,
    local_sem,
):
    cells, channels, points = src.shape
    me = lax.axis_index("cells")
    lanes = lax.broadcasted_iota(jnp.int32, (1, points), 1)
    cell_row = lax.broadcasted_iota(jnp.int32, (cells, points), 0)
    top = 3 * channels

    barrier = pltpu.get_barrier_semaphore()

    def greet(peer, _):
        pl.semaphore_signal(barrier, inc=1, device_id=(peer,), device_id_type=MESH)

    each_peer(me, greet)

    def prepare(c, _):
        live = lanes < tgt_len[c]
        masked[c] = jnp.where(live, tgt[c].astype(jnp.float32), FAR).astype(jnp.bfloat16)
        x = src[c].astype(jnp.float32)
        for i, piece in enumerate(three_parts(x * UNIT)):
            xaug[c, i * channels : (i + 1) * channels] = piece.astype(jnp.bfloat16)
        norm = (-0.5 * UNIT) * jnp.sum(x * x, axis=0, keepdims=True)
        xnorm[c] = norm
        xaug[c, top : top + AUX] = aux_rows(0, norm, points)
        return 0


    device_row = lax.broadcasted_iota(jnp.int32, (n, 128), 0)
    on_diagonal = device_row == lax.broadcasted_iota(jnp.int32, (n, 128), 1)

    def ask(c, table):
        for k in range(LIST - 1):
            wanted = near[k, c]
            entry = (c * 8 + k) * 16 + jnp.bitwise_and(wanted, 15)
            table = jnp.where(device_row == lax.shift_right_logical(wanted, 4), entry, table)
        return table

    table = lax.fori_loop(0, cells, ask, jnp.full((n, 128), -1, jnp.int32))
    asked[...] = table.reshape(n, 1, 128)

    def to_scalars(diagonal_of, at):
        row_ids[at] = jnp.sum(jnp.where(on_diagonal, diagonal_of, 0), axis=0, keepdims=True)
        copy = pltpu.make_async_copy(row_ids.at[at], ids.at[at], local_sem)
        copy.start()
        copy.wait()

    pl.semaphore_wait(barrier, n - 1)

    def send(outgoing, incoming, sem):
        def go(peer, _):
            pltpu.make_async_remote_copy(
                src_ref=outgoing.at[peer],
                dst_ref=incoming.at[me],
                send_sem=send_sems.at[sem],
                recv_sem=recv_sems.at[sem],
                device_id=(peer,),
                device_id_type=MESH,
            ).start()

        each_peer(me, go)

    def arrival(outgoing, incoming, first, count, send_sem, recv_sem):
        return pltpu.make_async_remote_copy(
            src_ref=outgoing.at[pl.ds(0, count)],
            dst_ref=incoming.at[pl.ds(first, count)],
            send_sem=send_sem,
            recv_sem=recv_sem,
            device_id=(lax.rem(me + 1, n),),
            device_id_type=MESH,
        )

    def finish(outgoing, incoming, sem):
        every = arrival(outgoing, incoming, 0, n - 1, send_sems.at[sem], recv_sems.at[sem])
        every.wait_recv()
        every.wait_send()

    send(asked, heard, 0)
    lax.fori_loop(0, cells, prepare, 0, unroll=2)
    to_scalars(table, 0)
    heard[me] = asked[me]
    finish(asked, heard, 0)
    to_scalars(heard[...].reshape(n, 128), 1)

    def entry_of(p):
        return lax.shift_right_logical(jnp.maximum(ids[0, 0, p], 0), 4)

    def cell_for(p):
        return jnp.bitwise_and(ids[1, 0, p], 15)

    packed = heard[...].reshape(n, 128)
    asker_cell = jnp.where(packed < 0, -1, jnp.bitwise_and(packed, 15))
    lane_of = lax.broadcasted_iota(jnp.int32, (n, 128), 1)
    to_cell = jnp.where(asker_cell == lane_of, 1.0, 0.0).astype(jnp.bfloat16)
    in_parts = jnp.logical_and(asker_cell == jnp.bitwise_and(lane_of, 15), lane_of < 3 * cells)
    from_parts = jnp.where(in_parts, 1.0, 0.0).astype(jnp.bfloat16)

    def for_askers(rows):
        parts = list(three_parts(rows)) + [jnp.zeros((128 - 3 * cells, points), jnp.float32)]
        stacked = jnp.concatenate(parts, axis=0).astype(jnp.bfloat16)
        return jnp.dot(from_parts, stacked, preferred_element_type=jnp.float32)

    x, z, y, core = coordinates(me)
    near_here = [lax.rem(y + dy, 4) * 2 + lax.rem(core + dc, 2) for dy in (2, 1, 3, 0) for dc in range(2)]
    home = x * 32 + z * 8

    def pick_plane(base):
        for j in range(8):
            send_feat[base + j] = masked[cell_for(base + j)]

    def send_plane(base, i, others):
        for j in others:
            pltpu.make_async_remote_copy(
                src_ref=send_feat.at[base + near_here[j]],
                dst_ref=got_feat.at[me],
                send_sem=send_sems.at[1],
                recv_sem=feat_sems.at[i],
                device_id=(base + near_here[j],),
                device_id_type=MESH,
            ).start()

    def pick_then_send(i, _):
        pick_plane(plane_of(x, z, i, 1, False))
        send_plane(plane_of(x, z, i - 1, 1, False), i - 1, range(8))
        return 0

    pick_plane(home)
    pick_plane(plane_of(x, z, 1, 1, False))
    send_plane(home, 0, (0, 1, 2, 3, 4, 5, 7))
    lax.fori_loop(2, 16, pick_then_send, 0)
    send_plane(plane_of(x, z, 15, 1, False), 15, range(8))
    got_feat[me] = masked[0]

    def place(block, spread, norms, at):
        for i in range(3):
            spread[at, i * channels : (i + 1) * channels] = block
        wide = block.astype(jnp.float32)
        norm = (-0.5 * UNIT) * jnp.sum(wide * wide, axis=0, keepdims=True)
        norms[at] = norm
        spread[at, top : top + AUX] = aux_rows(3, norm, points)

    def first_own(g, _):
        for j in range(8):
            c = g * 8 + j
            place(masked[c], yown, yown_norm, c)
            lse_own[c] = column_lse(yown[c], xaug[c])
        return 0

    lax.fori_loop(0, cells // 8, first_own, 0)


    def first_slots(i, _):
        base = plane_of(x, z, i, -1, False)
        arrival(send_feat, got_feat, base, 8, send_sems.at[1], feat_sems.at[i]).wait_recv()
        slots(base)
        return 0

    def slots(base):
        for j in range(8):
            slot = base + j
            place(got_feat[slot], yslot, yslot_norm, slot)
            cell = lax.shift_right_logical(entry_of(slot), 3)
            lse_slot[slot] = column_lse(yslot[slot], xaug[cell])

    arrival(send_feat, got_feat, home, 7, send_sems.at[1], feat_sems.at[0]).wait_recv()
    slots(home)
    lax.fori_loop(1, 16, first_slots, 0)
    arrival(send_feat, got_feat, 0, n - 1, send_sems.at[1], feat_sems.at[0]).wait_send()

    def slot_of(c, k):
        return lax.shift_right_logical(near[k, c], 4)

    def stack(rows):
        return jnp.concatenate([rows[c] for c in range(cells)], axis=0)

    for iteration in range(ITERS):
        last = iteration == ITERS - 1

        if iteration > 0:

            def second_rows(g, _):
                for j in range(8):
                    c = g * 8 + j
                    for k in range(LIST - 1):
                        slot = slot_of(c, k)
                        aux = aux_rows(3, yslot_norm[slot] + got_pot[slot], points)
                        block = jnp.concatenate([yslot[slot][:top], aux], axis=0)
                        lse_slot[c * 8 + k] = column_lse(block, xaug[c])
                return 0

            lax.fori_loop(0, cells // 8, second_rows, 0)

        def source_update(c, _):
            if iteration == 0:
                terms = [lse_slot[slot_of(c, k)] for k in range(LIST - 1)] + [lse_own[c]]
            else:
                terms = [lse_slot[c * 8 + k] for k in range(LIST - 1)] + [lse_own[c]]
            peak = functools.reduce(jnp.maximum, terms)
            total = sum(jnp.exp2(term - peak) for term in terms)
            live = lanes < src_len[c]
            pot = jnp.where(live, -damping * (peak + jnp.log2(total)), 0.0)
            if last:
                pots[c] = pot
            xaug[c, top : top + AUX] = aux_rows(0, jnp.where(live, pot + xnorm[c], NEVER), points)
            return 0

        lax.fori_loop(0, cells, source_update, 0, unroll=8)

        def columns(g, _):
            for j in range(8):
                c = g * 8 + j
                for k in range(LIST - 1):
                    part[c * 8 + k] = column_lse(xaug[c], yslot[slot_of(c, k)])
            return 0

        lax.fori_loop(0, cells // 8, columns, 0)

        def pick_parts(p, _):
            send_part[iteration, p] = part[entry_of(p)]
            return 0

        lax.fori_loop(0, n, pick_parts, 0, unroll=8)
        send(send_part.at[iteration], got_part.at[iteration], 2 + 2 * iteration)

        def own_columns(g, _):
            for j in range(8):
                lse_own[g * 8 + j] = column_lse(xaug[g * 8 + j], yown[g * 8 + j])
            return 0

        lax.fori_loop(0, cells // 8, own_columns, 0)
        if last:
            source_out[...] = stack(pots)
        own = stack(lse_own)
        finish(send_part.at[iteration], got_part.at[iteration], 2 + 2 * iteration)

        terms = got_part[iteration].reshape(n, points)
        asker = jnp.concatenate([asker_cell] * (points // 128), axis=1)
        best = [
            jnp.max(jnp.where(asker == c, terms, LOWEST), axis=0, keepdims=True)
            for c in range(cells)
        ]
        largest = jnp.maximum(own, jnp.concatenate(best, axis=0))
        shifted = jnp.where(asker >= 0, jnp.exp2(terms - for_askers(largest)), 0.0)
        arrived = sum(cross(to_cell, piece.astype(jnp.bfloat16)) for piece in three_parts(shifted))
        totals = jnp.exp2(own - largest) + arrived[:cells]
        lengths = jnp.zeros((cells, points), jnp.int32)
        for c in range(cells):
            lengths = jnp.where(cell_row == c, tgt_len[c], lengths)
        live = lax.broadcasted_iota(jnp.int32, (cells, points), 1) < lengths
        target = jnp.where(live, -damping * (largest + jnp.log2(totals)), 0.0)
        if last:
            target_out[...] = target
        else:
            for c in range(cells):
                pots[c] = target[c : c + 1]
            send_pot[...] = for_askers(target).reshape(n, 1, points)
            send(send_pot, got_pot, 3)

            def own_rows(g, _):
                for j in range(8):
                    c = g * 8 + j
                    xaug[c, top : top + AUX] = aux_rows(0, xnorm[c], points)
                    aux = aux_rows(3, yown_norm[c] + pots[c], points)
                    block = jnp.concatenate([yown[c][:top], aux], axis=0)
                    lse_own[c] = column_lse(block, xaug[c])
                return 0

            lax.fori_loop(0, cells // 8, own_rows, 0)
            finish(send_pot, got_pot, 3)


def local(src_feat, tgt_feat, src_len, tgt_len, neighbours):
    cells, channels, points = src_feat.shape
    n = lax.axis_size("cells")
    vmem = pl.BlockSpec(memory_space=pltpu.VMEM)
    smem = pl.BlockSpec(memory_space=pltpu.SMEM)
    deep = 3 * channels + AUX
    f32, bf16 = jnp.float32, jnp.bfloat16
    potentials = pl.pallas_call(
        functools.partial(kernel, n),
        name="sinkhorn",
        out_shape=(jax.ShapeDtypeStruct((cells, points), f32),) * 2,
        in_specs=[vmem, vmem, smem, smem, smem],
        out_specs=(vmem, vmem),
        scratch_shapes=[
            pltpu.VMEM((cells, channels, points), bf16),
            pltpu.VMEM((n, 1, 128), jnp.int32),
            pltpu.VMEM((n, 1, 128), jnp.int32),
            pltpu.VMEM((2, 1, 128), jnp.int32),
            pltpu.SMEM((2, 1, 128), jnp.int32),
            pltpu.VMEM((n, channels, points), bf16),
            pltpu.VMEM((n, channels, points), bf16),
            pltpu.VMEM((cells, deep, points), bf16),
            pltpu.VMEM((cells, 1, points), f32),
            pltpu.VMEM((cells, deep, points), bf16),
            pltpu.VMEM((cells, 1, points), f32),
            pltpu.VMEM((n, deep, points), bf16),
            pltpu.VMEM((n, 1, points), f32),
            pltpu.VMEM((cells, 1, points), f32),
            pltpu.VMEM((n, 1, points), f32),
            pltpu.VMEM((cells * 8, 1, points), f32),
            pltpu.VMEM((cells, 1, points), f32),
            pltpu.VMEM((ITERS, n, 1, points), f32),
            pltpu.VMEM((ITERS, n, 1, points), f32),
            pltpu.VMEM((n, 1, points), f32),
            pltpu.VMEM((n, 1, points), f32),
            pltpu.SemaphoreType.DMA((5,)),
            pltpu.SemaphoreType.DMA((5,)),
            pltpu.SemaphoreType.DMA((16,)),
            pltpu.SemaphoreType.DMA(()),
        ],
        compiler_params=pltpu.CompilerParams(
            collective_id=0, has_side_effects=True, vmem_limit_bytes=56 * 2**20
        ),
    )(src_feat, tgt_feat, src_len, tgt_len, neighbours.T)
    return tuple(potential * (1.0 / UNIT) for potential in potentials)


def solution(mesh):
    split = P("cells")
    return jax.shard_map(
        local,
        mesh=mesh,
        in_specs=(split,) * 5,
        out_specs=(split, split),
        check_vma=False,
    )
```

```python
import functools
import math

import jax
import jax.numpy as jnp
from jax import lax
from jax.experimental import pallas as pl
from jax.experimental.pallas import tpu as pltpu
from jax.sharding import PartitionSpec as P

MESH = pl.DeviceIdType.MESH
ITERS = 2
LIST = 6
entropy_scale = 0.5
marginal_weight = 1.0
damping = marginal_weight / (marginal_weight + entropy_scale)
UNIT = math.log2(math.e) / entropy_scale
NEVER = -1.0e30
LOWEST = -3.0e38
FAR = 2.0**50
AUX = 16


def coordinates(me):
    return lax.div(me, 32), lax.rem(lax.div(me, 8), 4), lax.rem(lax.div(me, 2), 4), lax.rem(me, 2)


def plane_of(x, z, i, sign, far_first):
    if far_first:
        dx, dz = 6 - lax.div(i, 4), 6 - lax.rem(i, 4)
    else:
        k = lax.rem(i * 5, 16)
        dx, dz = lax.div(k, 4), lax.rem(k, 4)
    if sign < 0:
        dx, dz = 4 - dx, 4 - dz
    return lax.rem(x + dx, 4) * 32 + lax.rem(z + dz, 4) * 8


def each_peer(me, act, far_first=True):
    x, z, y, core = coordinates(me)
    near = [lax.rem(y + dy, 4) * 2 + lax.rem(core + dc, 2) for dy in (2, 1, 3, 0) for dc in range(2)]

    def plane(i, _):
        base = plane_of(x, z, i, 1, far_first)
        for j in range(8):
            act(base + near[j], i)
        return 0

    def home(i):
        for j in (0, 1, 2, 3, 4, 5, 7):
            act(x * 32 + z * 8 + near[j], i)

    if far_first:
        lax.fori_loop(0, 10, plane, 0)
        lax.fori_loop(11, 16, plane, 0)
        home(10)
    else:
        home(0)
        lax.fori_loop(1, 16, plane, 0)


def three_parts(value):
    high = value.astype(jnp.bfloat16).astype(jnp.float32)
    rest = value - high
    middle = rest.astype(jnp.bfloat16).astype(jnp.float32)
    return high, middle, rest - middle


def aux_rows(first, value, points):
    row = lax.broadcasted_iota(jnp.int32, (AUX, points), 0)
    rows = jnp.where(row < 6, 1.0, 0.0)
    for i, piece in enumerate(three_parts(value)):
        rows = jnp.where(row == first + i, piece, rows)
    return rows.astype(jnp.bfloat16)


def cross(a, b):
    return lax.dot_general(a, b, (((0,), (0,)), ((), ())), preferred_element_type=jnp.float32)


def column_lse(a, b):
    half = b.shape[1] // 2
    terms = []
    for columns in (slice(0, half), slice(half, 2 * half)):
        block = cross(a, b[:, columns])
        peak = jnp.max(block, axis=0, keepdims=True)
        terms.append(peak + jnp.log2(jnp.sum(jnp.exp2(block - peak), axis=0, keepdims=True)))
    return jnp.concatenate(terms, axis=1)


def kernel(
    n,
    src,
    tgt,
    src_len,
    tgt_len,
    near,
    source_out,
    target_out,
    masked,
    asked,
    heard,
    row_ids,
    ids,
    send_feat,
    got_feat,
    xaug,
    xnorm,
    yown,
    yown_norm,
    yslot,
    yslot_norm,
    lse_own,
    lse_slot,
    part,
    pots,
    send_part,
    got_part,
    send_pot,
    got_pot,
    send_sems,
    recv_sems,
    feat_sems,
    local_sem,
):
    cells, channels, points = src.shape
    me = lax.axis_index("cells")
    lanes = lax.broadcasted_iota(jnp.int32, (1, points), 1)
    cell_row = lax.broadcasted_iota(jnp.int32, (cells, points), 0)
    top = 3 * channels

    barrier = pltpu.get_barrier_semaphore()

    def greet(peer, _):
        pl.semaphore_signal(barrier, inc=1, device_id=(peer,), device_id_type=MESH)

    each_peer(me, greet)

    def prepare(c, _):
        live = lanes < tgt_len[c]
        masked[c] = jnp.where(live, tgt[c].astype(jnp.float32), FAR).astype(jnp.bfloat16)
        x = src[c].astype(jnp.float32)
        for i, piece in enumerate(three_parts(x * UNIT)):
            xaug[c, i * channels : (i + 1) * channels] = piece.astype(jnp.bfloat16)
        norm = (-0.5 * UNIT) * jnp.sum(x * x, axis=0, keepdims=True)
        xnorm[c] = norm
        xaug[c, top : top + AUX] = aux_rows(0, norm, points)
        return 0


    device_row = lax.broadcasted_iota(jnp.int32, (n, 128), 0)
    on_diagonal = device_row == lax.broadcasted_iota(jnp.int32, (n, 128), 1)

    def ask(c, table):
        for k in range(LIST - 1):
            wanted = near[k, c]
            entry = (c * 8 + k) * 16 + jnp.bitwise_and(wanted, 15)
            table = jnp.where(device_row == lax.shift_right_logical(wanted, 4), entry, table)
        return table

    table = lax.fori_loop(0, cells, ask, jnp.full((n, 128), -1, jnp.int32))
    asked[...] = table.reshape(n, 1, 128)

    def to_scalars(diagonal_of, at):
        row_ids[at] = jnp.sum(jnp.where(on_diagonal, diagonal_of, 0), axis=0, keepdims=True)
        copy = pltpu.make_async_copy(row_ids.at[at], ids.at[at], local_sem)
        copy.start()
        copy.wait()

    pl.semaphore_wait(barrier, n - 1)

    def send(outgoing, incoming, sem):
        def go(peer, _):
            pltpu.make_async_remote_copy(
                src_ref=outgoing.at[peer],
                dst_ref=incoming.at[me],
                send_sem=send_sems.at[sem],
                recv_sem=recv_sems.at[sem],
                device_id=(peer,),
                device_id_type=MESH,
            ).start()

        each_peer(me, go)

    def arrival(outgoing, incoming, first, count, send_sem, recv_sem):
        return pltpu.make_async_remote_copy(
            src_ref=outgoing.at[pl.ds(0, count)],
            dst_ref=incoming.at[pl.ds(first, count)],
            send_sem=send_sem,
            recv_sem=recv_sem,
            device_id=(lax.rem(me + 1, n),),
            device_id_type=MESH,
        )

    def finish(outgoing, incoming, sem):
        every = arrival(outgoing, incoming, 0, n - 1, send_sems.at[sem], recv_sems.at[sem])
        every.wait_recv()
        every.wait_send()

    send(asked, heard, 0)
    lax.fori_loop(0, cells, prepare, 0, unroll=2)
    to_scalars(table, 0)
    heard[me] = asked[me]
    finish(asked, heard, 0)
    to_scalars(heard[...].reshape(n, 128), 1)

    def entry_of(p):
        return lax.shift_right_logical(jnp.maximum(ids[0, 0, p], 0), 4)

    def cell_for(p):
        return jnp.bitwise_and(ids[1, 0, p], 15)

    packed = heard[...].reshape(n, 128)
    asker_cell = jnp.where(packed < 0, -1, jnp.bitwise_and(packed, 15))
    lane_of = lax.broadcasted_iota(jnp.int32, (n, 128), 1)
    to_cell = jnp.where(asker_cell == lane_of, 1.0, 0.0).astype(jnp.bfloat16)
    in_parts = jnp.logical_and(asker_cell == jnp.bitwise_and(lane_of, 15), lane_of < 3 * cells)
    from_parts = jnp.where(in_parts, 1.0, 0.0).astype(jnp.bfloat16)

    def for_askers(rows):
        parts = list(three_parts(rows)) + [jnp.zeros((128 - 3 * cells, points), jnp.float32)]
        stacked = jnp.concatenate(parts, axis=0).astype(jnp.bfloat16)
        return jnp.dot(from_parts, stacked, preferred_element_type=jnp.float32)

    def pick_features(p, _):
        send_feat[p] = masked[cell_for(p)]
        return 0

    lax.fori_loop(0, n, pick_features, 0, unroll=8)

    def send_features(peer, i):
        pltpu.make_async_remote_copy(
            src_ref=send_feat.at[peer],
            dst_ref=got_feat.at[me],
            send_sem=send_sems.at[1],
            recv_sem=feat_sems.at[i],
            device_id=(peer,),
            device_id_type=MESH,
        ).start()

    each_peer(me, send_features, False)
    got_feat[me] = masked[0]

    def place(block, spread, norms, at):
        for i in range(3):
            spread[at, i * channels : (i + 1) * channels] = block
        wide = block.astype(jnp.float32)
        norm = (-0.5 * UNIT) * jnp.sum(wide * wide, axis=0, keepdims=True)
        norms[at] = norm
        spread[at, top : top + AUX] = aux_rows(3, norm, points)

    def first_own(g, _):
        for j in range(8):
            c = g * 8 + j
            place(masked[c], yown, yown_norm, c)
            lse_own[c] = column_lse(yown[c], xaug[c])
        return 0

    lax.fori_loop(0, cells // 8, first_own, 0)

    x, z, _, _ = coordinates(me)

    def first_slots(i, _):
        base = plane_of(x, z, i, -1, False)
        arrival(send_feat, got_feat, base, 8, send_sems.at[1], feat_sems.at[i]).wait_recv()
        slots(base)
        return 0

    def slots(base):
        for j in range(8):
            slot = base + j
            place(got_feat[slot], yslot, yslot_norm, slot)
            cell = lax.shift_right_logical(entry_of(slot), 3)
            lse_slot[slot] = column_lse(yslot[slot], xaug[cell])

    home = x * 32 + z * 8
    arrival(send_feat, got_feat, home, 7, send_sems.at[1], feat_sems.at[0]).wait_recv()
    slots(home)
    lax.fori_loop(1, 16, first_slots, 0)
    arrival(send_feat, got_feat, 0, n - 1, send_sems.at[1], feat_sems.at[0]).wait_send()

    def slot_of(c, k):
        return lax.shift_right_logical(near[k, c], 4)

    def stack(rows):
        return jnp.concatenate([rows[c] for c in range(cells)], axis=0)

    for iteration in range(ITERS):
        last = iteration == ITERS - 1

        if iteration > 0:

            def second_rows(g, _):
                for j in range(8):
                    c = g * 8 + j
                    for k in range(LIST - 1):
                        slot = slot_of(c, k)
                        aux = aux_rows(3, yslot_norm[slot] + got_pot[slot], points)
                        block = jnp.concatenate([yslot[slot][:top], aux], axis=0)
                        lse_slot[c * 8 + k] = column_lse(block, xaug[c])
                return 0

            lax.fori_loop(0, cells // 8, second_rows, 0)

        def source_update(c, _):
            if iteration == 0:
                terms = [lse_slot[slot_of(c, k)] for k in range(LIST - 1)] + [lse_own[c]]
            else:
                terms = [lse_slot[c * 8 + k] for k in range(LIST - 1)] + [lse_own[c]]
            peak = functools.reduce(jnp.maximum, terms)
            total = sum(jnp.exp2(term - peak) for term in terms)
            live = lanes < src_len[c]
            pot = jnp.where(live, -damping * (peak + jnp.log2(total)), 0.0)
            if last:
                pots[c] = pot
            xaug[c, top : top + AUX] = aux_rows(0, jnp.where(live, pot + xnorm[c], NEVER), points)
            return 0

        lax.fori_loop(0, cells, source_update, 0, unroll=8)

        def columns(g, _):
            for j in range(8):
                c = g * 8 + j
                for k in range(LIST - 1):
                    part[c * 8 + k] = column_lse(xaug[c], yslot[slot_of(c, k)])
            return 0

        lax.fori_loop(0, cells // 8, columns, 0)

        def pick_parts(p, _):
            send_part[iteration, p] = part[entry_of(p)]
            return 0

        lax.fori_loop(0, n, pick_parts, 0, unroll=8)
        send(send_part.at[iteration], got_part.at[iteration], 2 + 2 * iteration)

        def own_columns(g, _):
            for j in range(8):
                lse_own[g * 8 + j] = column_lse(xaug[g * 8 + j], yown[g * 8 + j])
            return 0

        lax.fori_loop(0, cells // 8, own_columns, 0)
        if last:
            source_out[...] = stack(pots)
        own = stack(lse_own)
        finish(send_part.at[iteration], got_part.at[iteration], 2 + 2 * iteration)

        terms = got_part[iteration].reshape(n, points)
        asker = jnp.concatenate([asker_cell] * (points // 128), axis=1)
        best = [
            jnp.max(jnp.where(asker == c, terms, LOWEST), axis=0, keepdims=True)
            for c in range(cells)
        ]
        largest = jnp.maximum(own, jnp.concatenate(best, axis=0))
        shifted = jnp.where(asker >= 0, jnp.exp2(terms - for_askers(largest)), 0.0)
        arrived = sum(cross(to_cell, piece.astype(jnp.bfloat16)) for piece in three_parts(shifted))
        totals = jnp.exp2(own - largest) + arrived[:cells]
        lengths = jnp.zeros((cells, points), jnp.int32)
        for c in range(cells):
            lengths = jnp.where(cell_row == c, tgt_len[c], lengths)
        live = lax.broadcasted_iota(jnp.int32, (cells, points), 1) < lengths
        target = jnp.where(live, -damping * (largest + jnp.log2(totals)), 0.0)
        if last:
            target_out[...] = target
        else:
            for c in range(cells):
                pots[c] = target[c : c + 1]
            send_pot[...] = for_askers(target).reshape(n, 1, points)
            send(send_pot, got_pot, 3)

            def own_rows(g, _):
                for j in range(8):
                    c = g * 8 + j
                    xaug[c, top : top + AUX] = aux_rows(0, xnorm[c], points)
                    aux = aux_rows(3, yown_norm[c] + pots[c], points)
                    block = jnp.concatenate([yown[c][:top], aux], axis=0)
                    lse_own[c] = column_lse(block, xaug[c])
                return 0

            lax.fori_loop(0, cells // 8, own_rows, 0)
            finish(send_pot, got_pot, 3)


def local(src_feat, tgt_feat, src_len, tgt_len, neighbours):
    cells, channels, points = src_feat.shape
    n = lax.axis_size("cells")
    vmem = pl.BlockSpec(memory_space=pltpu.VMEM)
    smem = pl.BlockSpec(memory_space=pltpu.SMEM)
    deep = 3 * channels + AUX
    f32, bf16 = jnp.float32, jnp.bfloat16
    potentials = pl.pallas_call(
        functools.partial(kernel, n),
        name="sinkhorn",
        out_shape=(jax.ShapeDtypeStruct((cells, points), f32),) * 2,
        in_specs=[vmem, vmem, smem, smem, smem],
        out_specs=(vmem, vmem),
        scratch_shapes=[
            pltpu.VMEM((cells, channels, points), bf16),
            pltpu.VMEM((n, 1, 128), jnp.int32),
            pltpu.VMEM((n, 1, 128), jnp.int32),
            pltpu.VMEM((2, 1, 128), jnp.int32),
            pltpu.SMEM((2, 1, 128), jnp.int32),
            pltpu.VMEM((n, channels, points), bf16),
            pltpu.VMEM((n, channels, points), bf16),
            pltpu.VMEM((cells, deep, points), bf16),
            pltpu.VMEM((cells, 1, points), f32),
            pltpu.VMEM((cells, deep, points), bf16),
            pltpu.VMEM((cells, 1, points), f32),
            pltpu.VMEM((n, deep, points), bf16),
            pltpu.VMEM((n, 1, points), f32),
            pltpu.VMEM((cells, 1, points), f32),
            pltpu.VMEM((n, 1, points), f32),
            pltpu.VMEM((cells * 8, 1, points), f32),
            pltpu.VMEM((cells, 1, points), f32),
            pltpu.VMEM((ITERS, n, 1, points), f32),
            pltpu.VMEM((ITERS, n, 1, points), f32),
            pltpu.VMEM((n, 1, points), f32),
            pltpu.VMEM((n, 1, points), f32),
            pltpu.SemaphoreType.DMA((5,)),
            pltpu.SemaphoreType.DMA((5,)),
            pltpu.SemaphoreType.DMA((16,)),
            pltpu.SemaphoreType.DMA(()),
        ],
        compiler_params=pltpu.CompilerParams(
            collective_id=0, has_side_effects=True, vmem_limit_bytes=56 * 2**20
        ),
    )(src_feat, tgt_feat, src_len, tgt_len, neighbours.T)
    return tuple(potential * (1.0 / UNIT) for potential in potentials)


def solution(mesh):
    split = P("cells")
    return jax.shard_map(
        local,
        mesh=mesh,
        in_specs=(split,) * 5,
        out_specs=(split, split),
        check_vma=False,
    )
```
